512 devices in a mesh: kv: 4 (over x), blk: 128 (over y, z, core).
Axes of the slice: x: 4, y: 8, z: 8, core: 2. Of those that a mesh axis runs over, the one named last changes fastest.
Arguments:
- residual: bfloat16 [512, 2560], P('blk'), may hold values from -12 to 12
- queries: bfloat16 [512, 1536], P('blk', 'kv'), may hold values from -10 to 10
- new_kv: bfloat16 [512, 1024], P('blk', 'kv'), may hold values from -4 to 4
- suffix_kv: bfloat16 [128, 4, 128, 256], P('blk', 'kv'), may hold values from -4 to 4
- suffix_len: int32 [128], P('blk'), may hold values from 1 to 128, 8192 in all
- shared_kv: bfloat16 [2048, 4, 128, 256], P('blk', 'kv'), may hold values from -4 to 4
- block_node: int32 [2048], P('blk'), may hold values from 0 to 111, as said below
- block_len: int32 [2048], P('blk'), may hold values from 1 to 128
- group_root: int32 [96], replicated, may hold values from 0 to 15, as said below
- request_group: int32 [128], replicated, may hold values from 0 to 95, as said below
- out_weight: bfloat16 [1536, 2560], P('kv'), may hold values from -0.15625 to 0.15625
- norm_gain: float32 [2560], replicated, may hold values from 0.1 to 1.9
- router: bfloat16 [2560, 32], replicated, may hold values from -0.125 to 0.125
- routes: int32 [512, 6], P('blk'), may hold values from 0 to 31, all different within a row; in each aligned block of 4 rows (0 to 3, 4 to 7, ...) at most 2 rows name the same one
- expert_gate_up: bfloat16 [128, 2560, 768], P('blk', 'kv'), may hold values from -0.125 to 0.125
- expert_down: bfloat16 [128, 384, 2560], P('blk', None, 'kv'), may hold values from -0.15625 to 0.15625
Outputs:
- attention: bfloat16 [512, 1536], P('blk', 'kv')
- layer_out: bfloat16 [512, 2560], P('blk', 'kv')
The draws below stay inside these ranges and needn't reach their ends.
Inputs may be any that keep to these rules, and one draw needn't show every extreme that they name: `group_root`: groups never fall from one group to the next, so that the groups of one root are consecutive. `request_group`: groups never fall from one request to the next, so that the requests under one node are consecutive. `block_node`: every root owns at least one shared block. `routes`: among the rows of one index of blk no expert is named more than 2 times.
All inputs are finite; a program needn't handle non-finite values. No bound on the sum of `suffix_len` on one device may be relied on, other than what follows from the above.
Results may differ from the reference program's by a relative error of at most 0.018.
Values may be sent and summed in bfloat16 or wider, within the bound.
A program may use at most 64 MiB of HBM per device.

```python
import math
import jax
import jax.numpy as jnp
import numpy as np
from jax import lax

D = 2560
HD = 128
HQ = 12
KVH = 4
EXPERTS = 32
FF = 1536
TOPK = 6
NEW = 4
BLOCK = 128
ROOTS = 16
GROUPS = 96
SUF = 128
REQS = 128
TOK_DEV = 4
TOK = 512
NBLOCKS = 2048
SPLIT = 4
PIECES = 128
FFP = 384
CAP = 2
N_BLK = 128


def aligned_signs(key):
    coin_flips = jax.random.bernoulli(jax.random.fold_in(key, 71), 0.5, (KVH, HD))
    return jnp.where(coin_flips, 1.0, -1.0).astype(jnp.float32)


def draw_queries(key, part):
    group_heads = HQ // KVH
    base_draw = 2.5 * jnp.clip(jax.random.normal(jax.random.fold_in(key, 1), (TOK, HQ, HD), jnp.float32), -4.0, 4.0)
    head_signs = jnp.repeat(aligned_signs(key), group_heads, axis=0)
    row_index = jnp.arange(TOK)
    strength = 7.0 + 1.5 * (row_index // 5 % 3).astype(jnp.float32)
    chosen = row_index % 5 == 0
    aligned = strength[:, None, None] * head_signs[None, :, :]
    drawn = jnp.where(chosen[:, None, None], aligned, base_draw)
    return drawn.reshape(TOK, HQ * HD).astype(jnp.bfloat16)


def draw_shared_kv(key, part):
    full_shape = (NBLOCKS, KVH, BLOCK, 2 * HD)
    base_draw = jnp.clip(jax.random.normal(jax.random.fold_in(key, 2), full_shape, jnp.float32), -4.0, 4.0)
    sign_table = aligned_signs(key)
    position = jnp.arange(BLOCK)
    key_level = jnp.where(position == 0, 4.0, 3.96)
    planted = key_level[None, None, :, None] * sign_table[None, :, None, :]
    key_part = jnp.where((position < 2)[None, None, :, None], planted, base_draw[..., :HD])
    drawn = jnp.concatenate([key_part, base_draw[..., HD:]], axis=-1)
    return drawn.astype(jnp.bfloat16)


def draw_residual(key, part):
    row_scale = jnp.exp(jax.random.uniform(jax.random.fold_in(key, 3), (TOK, 1), jnp.float32, math.log(0.1), 0.0))
    col_scale = jnp.exp(jax.random.uniform(jax.random.fold_in(key, 4), (1, D), jnp.float32, math.log(0.3), math.log(3.0)))
    base_draw = jnp.clip(jax.random.normal(jax.random.fold_in(key, 5), (TOK, D), jnp.float32), -4.0, 4.0)
    return (base_draw * row_scale * col_scale).astype(jnp.bfloat16)


def draw_block_node(key, part):
    node_count = ROOTS + GROUPS
    position = jnp.arange(NBLOCKS, dtype=jnp.int32)
    spare_draw = jax.random.randint(jax.random.fold_in(key, 6), (NBLOCKS,), 0, 2 * node_count, dtype=jnp.int32)
    spare_node = jnp.where(spare_draw < node_count, spare_draw, spare_draw % ROOTS)
    labels = jnp.where(position < node_count, position, spare_node)
    shuffle = jax.random.permutation(jax.random.fold_in(key, 7), NBLOCKS)
    return labels[shuffle].astype(jnp.int32)


def draw_block_len(key, part):
    spare_draw = jax.random.randint(jax.random.fold_in(key, 8), (NBLOCKS,), 1, 2 * BLOCK, dtype=jnp.int32)
    return jnp.minimum(spare_draw, BLOCK).astype(jnp.int32)


def draw_group_root(key, part):
    spare_draw = jax.random.randint(jax.random.fold_in(key, 9), (GROUPS,), 0, ROOTS, dtype=jnp.int32)
    spare_draw = spare_draw.at[0].set(ROOTS - 1).at[1].set(0)
    return jnp.sort(spare_draw).astype(jnp.int32)


def draw_request_group(key, part):
    spare_draw = jax.random.randint(jax.random.fold_in(key, 10), (REQS,), 0, GROUPS, dtype=jnp.int32)
    spare_draw = spare_draw.at[0].set(GROUPS - 1).at[1].set(0)
    return jnp.sort(spare_draw).astype(jnp.int32)


def levels(key, shape, split, smallest, largest):
    def one(dim, blocks):
        heights = jax.random.uniform(jax.random.fold_in(jax.random.fold_in(key, 6), dim), (blocks,), jnp.float32, smallest / len(split), largest / len(split))
        return jnp.repeat(jnp.exp(heights), shape[dim] // blocks).reshape((-1,) + (1,) * (len(shape) - dim - 1))

    level = one(*split[0])
    for cut in split[1:]:
        level = level * one(*cut)
    return level


def length_profile(amount, total, reach, lean):
    weights = [(1 << 20) // math.isqrt(grade ** lean) + 1 for grade in range(2, amount + 1)]
    surplus, given = total - reach - (amount - 1), [1] * (amount - 1)
    while surplus > 0:
        candidates = [i for i in range(amount - 1) if given[i] < reach]
        pool, budget = sum([weights[i] for i in candidates]), surplus
        for i in candidates:
            more = min(reach - given[i], max(1, budget * weights[i] // pool), surplus)
            given[i] = given[i] + more
            surplus = surplus - more
    return np.array([reach] + given)


def uneven(rng, amount, total, limit, skew):
    if amount == 2:
        one = jax.random.randint(rng, (), max(1, total - limit), min(limit, total - 1) + 1)
        return jnp.stack([one, total - one])
    sizes = jnp.asarray(length_profile(amount, total, limit, skew), jnp.int32)
    pairs = (amount - 1) // 2
    donor, receiver = sizes[1:1 + 2 * pairs:2], sizes[2:2 + 2 * pairs:2]
    margin = jnp.minimum(donor - 1, limit - receiver)
    passed = jax.random.randint(jax.random.fold_in(rng, 1), (pairs,), 0, 1 << 20) % (margin + 1)
    sizes = sizes.at[1:1 + 2 * pairs:2].set(donor - passed).at[2:2 + 2 * pairs:2].set(receiver + passed)
    return sizes[jax.random.permutation(jax.random.fold_in(rng, 2), amount)]


def routed_block(stream_key, own, number, rows, count, top, most, skew):
    sequence = jax.random.permutation(stream_key, count)
    heavy_load, common = portions_of(count, rows * top, most, skew, True), portions_of(count, rows * top, most, skew, False)
    places = jnp.arange(count)

    def named(lengths, rotation):
        used = int((lengths > 0).sum())
        fixed = max(1, used // 4)
        moved = fixed + (places - fixed + rotation * (used - fixed)) % max(1, count - fixed)
        return jnp.zeros((count,), jnp.int32).at[sequence[jnp.where(places < fixed, places, moved)]].set(jnp.asarray(lengths, jnp.int32))

    lengths = jnp.where(number % 4 == 0, named(heavy_load, number // 4), named(common, number - number // 4 - 1))
    mixed = jax.random.permutation(jax.random.fold_in(own, 3), count)
    source_of, taker = mixed[0:count // 2 * 2:2], mixed[1:count // 2 * 2:2]
    slack = jnp.minimum(lengths[source_of] - 1, most - lengths[taker]) // 2
    slack = jnp.where((source_of == sequence[0]) | (taker == sequence[0]) | (lengths[taker] == 0), 0, jnp.maximum(slack, 0))
    moved = jax.random.randint(jax.random.fold_in(own, 4), (count // 2,), 0, 1 << 20) % (slack + 1)
    lengths = lengths.at[source_of].add(-moved).at[taker].add(moved)
    members = jnp.searchsorted(jnp.cumsum(lengths), jnp.arange(rows * top), side="right").astype(jnp.int32)
    grid = members.reshape(top, rows).T
    grid = grid[jax.random.permutation(jax.random.fold_in(own, 1), rows)]
    rotation = jax.random.randint(jax.random.fold_in(own, 2), (rows, 1), 0, top)
    return jnp.take_along_axis(grid, (jnp.arange(top)[None, :] + rotation) % top, axis=1)


def portions_of(amount, total, most, skew, full):
    portions = [(1 << 20) // math.isqrt(standing ** skew) + 1 for standing in range(1, amount + 1)]
    largest = most if full else min(most, max(-(-total // amount), total * portions[0] // sum(portions)))
    least = 1 if total - largest >= amount - 1 else 0
    given, rest = [largest] + [least] * (amount - 1), total - largest - least * (amount - 1)
    while rest > 0:
        candidates = [i for i in range(1, amount) if given[i] < largest] or [i for i in range(1, amount) if given[i] < most]
        mass, left = sum([portions[i] for i in candidates]), rest
        for i in candidates:
            extra = min(most - given[i], max(1, left * portions[i] // mass), rest)
            given[i] = given[i] + extra
            rest = rest - extra
    return np.array(given)


def normal_values(rng, dims, width, most, pieces=(), kind=jnp.bfloat16):
    level = levels(rng, dims, pieces, -0.22, 0.18) if pieces else 1.0
    values = jax.random.normal(rng, dims, jnp.float32) * width * level
    return jnp.minimum(jnp.maximum(values, -most), most).astype(kind)


def setup_inputs(seed: int = 0) -> dict:
    splits = jax.random.split(jax.random.key(seed), 17)
    residual = draw_residual(jax.random.fold_in(splits[16], 71), 0)
    queries = draw_queries(jax.random.fold_in(splits[16], 71), 0)
    new_kv = normal_values(splits[2], (TOK, KVH * 2 * HD), 1.0, 4.0, ((0, 128), (1, 4)))
    suffix_kv = normal_values(splits[3], (REQS, KVH, SUF, 2 * HD), 1.0, 4.0, ((0, 128), (1, 4)))
    suffix_len = uneven(splits[4], REQS, REQS * SUF // 2, SUF, 2).astype(jnp.int32)
    shared_kv = draw_shared_kv(jax.random.fold_in(splits[16], 71), 0)
    block_node = draw_block_node(jax.random.fold_in(splits[16], 71), 0)
    block_len = draw_block_len(jax.random.fold_in(splits[16], 71), 0)
    group_root = draw_group_root(jax.random.fold_in(splits[16], 71), 0)
    request_group = draw_request_group(jax.random.fold_in(splits[16], 71), 0)
    out_weight = normal_values(splits[10], (HQ * HD, D), (HQ * HD) ** -0.5, 0.15625, ((0, 4),))
    norm_gain = jnp.clip(1.0 + 0.18 * jax.random.normal(splits[11], (D,), jnp.float32), 0.1, 1.9)
    router = normal_values(splits[12], (D, EXPERTS), D ** -0.5, 0.125)
    routes_keys = jax.random.split(jax.random.fold_in(splits[13], 1), TOK // TOK_DEV)
    routes_turns = jax.random.permutation(jax.random.fold_in(splits[13], 3), TOK // TOK_DEV)
    routes = jax.vmap(lambda own, number: routed_block(jax.random.fold_in(splits[13], 2), own, number, TOK_DEV, EXPERTS, TOPK, CAP, 2))(routes_keys, routes_turns).reshape((TOK, TOPK))
    expert_gate_up = normal_values(splits[14], (PIECES, D, 2 * FFP), D ** -0.5, 0.125, ((0, 128), (1, 4)))
    expert_down = normal_values(splits[15], (PIECES, FFP, D), FF ** -0.5, 0.15625, ((0, 128), (2, 4)))
    return dict(residual=residual, queries=queries, new_kv=new_kv, suffix_kv=suffix_kv, suffix_len=suffix_len, shared_kv=shared_kv, block_node=block_node, block_len=block_len, group_root=group_root, request_group=request_group, out_weight=out_weight, norm_gain=norm_gain, router=router, routes=routes, expert_gate_up=expert_gate_up, expert_down=expert_down)


NEGATIVE = -1e+30
HIGHEST = lax.Precision.HIGHEST

def shared_pass(query_all, shared_kv, block_node, block_len, group_root, request_group):
    score_scale = 1.0 / math.sqrt(HD)
    window = min(32, REQS)
    row_span = window * NEW
    group_ids = jnp.arange(GROUPS, dtype=jnp.int32)
    root_of = lax.optimization_barrier(jnp.sum(jnp.where(request_group[:, None] == group_ids[None, :], group_root[None, :], 0), axis=1)).astype(jnp.int32)
    positions = jnp.arange(BLOCK, dtype=jnp.int32)
    offsets = jnp.arange(window, dtype=jnp.int32)

    def per_block(j, running):
        node_id = block_node[j]
        is_root = node_id < ROOTS
        range_low = jnp.where(is_root, jnp.sum((root_of < node_id).astype(jnp.int32)), jnp.sum((request_group < node_id - ROOTS).astype(jnp.int32))).astype(jnp.int32)
        range_high = jnp.where(is_root, jnp.sum((root_of <= node_id).astype(jnp.int32)), jnp.sum((request_group <= node_id - ROOTS).astype(jnp.int32))).astype(jnp.int32)
        block_rows = lax.dynamic_index_in_dim(shared_kv, j, 0, keepdims=False).astype(jnp.float32)
        block_keys = block_rows[:, :, :HD]
        block_values = block_rows[:, :, HD:]
        key_ok = positions < block_len[j]

        def keep_going(state_in):
            return state_in[0] < range_high

        def advance(state_in):
            start_req, row_tops, totals, outputs = state_in
            window_start = jnp.minimum(start_req, REQS - window).astype(jnp.int32)
            req_ids = window_start + offsets
            req_ok = jnp.repeat((req_ids >= start_req) & (req_ids < range_high), NEW)
            offset = window_start * NEW
            query_rows = lax.dynamic_slice_in_dim(query_all, offset, row_span, 0)
            scores = jnp.einsum('tkgd,kpd->tkgp', query_rows, block_keys, precision=HIGHEST) * score_scale
            is_valid = req_ok[:, None, None, None] & key_ok[None, None, None, :]
            scores = jnp.where(is_valid, scores, NEGATIVE)
            old_top = lax.dynamic_slice_in_dim(row_tops, offset, row_span, 0)
            old_total = lax.dynamic_slice_in_dim(totals, offset, row_span, 0)
            old_out = lax.dynamic_slice_in_dim(outputs, offset, row_span, 0)
            new_top = jnp.maximum(old_top, lax.optimization_barrier(jnp.max(scores, axis=3)))
            weights = jnp.where(is_valid, jnp.exp(scores - new_top[..., None]), 0.0)
            shrink = jnp.exp(old_top - new_top)
            new_total = old_total * shrink + lax.optimization_barrier(jnp.sum(weights, axis=3))
            new_out = old_out * shrink[..., None] + jnp.einsum('tkgp,kpd->tkgd', weights, block_values, precision=HIGHEST)
            row_tops = lax.dynamic_update_slice_in_dim(row_tops, new_top, offset, 0)
            totals = lax.dynamic_update_slice_in_dim(totals, new_total, offset, 0)
            outputs = lax.dynamic_update_slice_in_dim(outputs, new_out, offset, 0)
            return (window_start + window, row_tops, totals, outputs)
        finished = lax.while_loop(keep_going, advance, (range_low,) + running)
        return finished[1:]
    group_heads = HQ // KVH
    initial = (jnp.full((TOK, KVH, group_heads), NEGATIVE, jnp.float32), jnp.zeros((TOK, KVH, group_heads), jnp.float32), jnp.zeros((TOK, KVH, group_heads, HD), jnp.float32))
    return lax.fori_loop(0, NBLOCKS, per_block, initial)

def reference(residual, queries, new_kv, suffix_kv, suffix_len, shared_kv, block_node, block_len, group_root, request_group, out_weight, norm_gain, router, routes, expert_gate_up, expert_down):
    group_heads = HQ // KVH
    score_scale = 1.0 / math.sqrt(HD)
    query_all = queries.astype(jnp.float32).reshape(TOK, KVH, group_heads, HD)
    shared_top, shared_total, shared_out = shared_pass(query_all, shared_kv, block_node, block_len, group_root, request_group)
    query_req = query_all.reshape(REQS, NEW, KVH, group_heads, HD)
    suffix_rows = suffix_kv.astype(jnp.float32)
    suffix_scores = jnp.einsum('rikgd,rkpd->rikgp', query_req, suffix_rows[..., :HD], precision=HIGHEST) * score_scale
    suffix_ok = (jnp.arange(SUF, dtype=jnp.int32)[None, :] < suffix_len[:, None])[:, None, None, None, :]
    suffix_scores = jnp.where(suffix_ok, suffix_scores, NEGATIVE)
    new_rows = new_kv.astype(jnp.float32).reshape(REQS, NEW, KVH, 2 * HD)
    fresh_scores = jnp.einsum('rikgd,rjkd->rikgj', query_req, new_rows[..., :HD], precision=HIGHEST) * score_scale
    step_ids = jnp.arange(NEW, dtype=jnp.int32)
    causal = (step_ids[None, :] <= step_ids[:, None])[None, :, None, None, :]
    fresh_scores = jnp.where(causal, fresh_scores, NEGATIVE)
    shared_top = shared_top.reshape(REQS, NEW, KVH, group_heads)
    shared_total = shared_total.reshape(REQS, NEW, KVH, group_heads)
    shared_out = shared_out.reshape(REQS, NEW, KVH, group_heads, HD)
    row_top = jnp.maximum(shared_top, jnp.maximum(lax.optimization_barrier(jnp.max(suffix_scores, axis=4)), lax.optimization_barrier(jnp.max(fresh_scores, axis=4))))
    suffix_weights = jnp.where(suffix_ok, jnp.exp(suffix_scores - row_top[..., None]), 0.0)
    fresh_weights = jnp.where(causal, jnp.exp(fresh_scores - row_top[..., None]), 0.0)
    shared_factor = jnp.exp(shared_top - row_top)
    denominator = shared_total * shared_factor + lax.optimization_barrier(jnp.sum(suffix_weights, axis=4)) + lax.optimization_barrier(jnp.sum(fresh_weights, axis=4))
    numerator = shared_out * shared_factor[..., None] + jnp.einsum('rikgp,rkpd->rikgd', suffix_weights, suffix_rows[..., HD:], precision=HIGHEST) + jnp.einsum('rikgj,rjkd->rikgd', fresh_weights, new_rows[..., HD:], precision=HIGHEST)
    attention = (numerator / denominator[..., None]).reshape(TOK, HQ * HD).astype(jnp.bfloat16)
    projected = jnp.dot(attention, out_weight, preferred_element_type=jnp.float32)
    stream = residual.astype(jnp.float32) + projected
    normed = (stream * lax.rsqrt(lax.optimization_barrier(jnp.mean(stream * stream, axis=1, keepdims=True)) + 1e-06) * norm_gain).astype(jnp.bfloat16)
    logits = jnp.dot(normed, router, preferred_element_type=jnp.float32)
    expert_ids = jnp.arange(EXPERTS, dtype=jnp.int32)
    chosen = lax.optimization_barrier(jnp.sum(jnp.where(routes[:, :, None] == expert_ids[None, None, :], logits[:, None, :], 0.0), axis=2))
    gate_values = jax.nn.sigmoid(chosen)
    weights = gate_values / lax.optimization_barrier(jnp.sum(gate_values, axis=1, keepdims=True))
    flat_routes = routes.reshape(-1)
    sorted_rows = jnp.argsort(flat_routes, stable=True).astype(jnp.int32)
    counts = lax.optimization_barrier(jnp.sum((flat_routes[:, None] == expert_ids[None, :]).astype(jnp.int32), axis=0)).astype(jnp.int32)
    starts = (jnp.cumsum(counts) - counts).astype(jnp.int32)
    row_bound = N_BLK * CAP
    padded = jnp.concatenate([sorted_rows, jnp.zeros((row_bound,), jnp.int32)])
    flat_weights = weights.reshape(-1)

    def per_expert(e, summed):
        row_ids = lax.dynamic_slice_in_dim(padded, starts[e], row_bound, 0)
        live_rows = jnp.arange(row_bound, dtype=jnp.int32) < counts[e]
        token_ids = row_ids // TOPK
        inputs = normed[token_ids].astype(jnp.float32)
        gate_up = lax.dynamic_slice_in_dim(expert_gate_up, e * SPLIT, SPLIT, 0).astype(jnp.float32)
        mixed = jnp.einsum('nd,pdf->npf', inputs, gate_up, precision=HIGHEST)
        hidden = (jax.nn.silu(mixed[..., :FFP]) * mixed[..., FFP:]).astype(jnp.bfloat16)
        hidden = lax.optimization_barrier(hidden).astype(jnp.float32)
        down = lax.dynamic_slice_in_dim(expert_down, e * SPLIT, SPLIT, 0).astype(jnp.float32)
        result = jnp.einsum('npf,pfd->nd', hidden, down, precision=HIGHEST)
        result = result * jnp.where(live_rows, flat_weights[row_ids], 0.0)[:, None]
        return summed.at[token_ids].add(result)
    expert_sum = lax.fori_loop(0, EXPERTS, per_expert, jnp.zeros((TOK, D), jnp.float32))
    layer_out = (stream + expert_sum).astype(jnp.bfloat16)
    return (attention, layer_out)
```

```python
import math

import jax
import jax.numpy as jnp
from jax import lax
from jax.experimental import pallas as pl
from jax.experimental.pallas import tpu as pltpu
from jax.sharding import PartitionSpec as P

MESH = pl.DeviceIdType.MESH
F32 = jnp.float32
BF16 = jnp.bfloat16
I32 = jnp.int32

HD = 128
NEW = 4
HEADS = 3
TOPK = 6
ROOTS = 16
EXPERTS = 32
NY, NZ = 8, 8
NC = NY * NZ
NX = 4
BLOCKS = 16
KEYS = BLOCKS * 128
D = 2560
Q4 = 640
FFP = 384
ROWS = 16
SLOTS = NC * 2
GRP = Q4 // 128
BIG = 16384.0
UNSEEN = -65536.0
SCALE = 1.0 / math.sqrt(HD)
LOG2E = 1.4426950408889634
SPAN = 512
SRC = 72


def iota(shape, dim):
    return lax.broadcasted_iota(I32, shape, dim)


def mm(a, b):
    return jnp.dot(a, b, preferred_element_type=F32)


def mmt(a, b):
    return lax.dot_general(a, b, (((1,), (1,)), ((), ())), preferred_element_type=F32)


def flag(cond):
    return jnp.where(cond, 1.0, 0.0).astype(BF16)


def tile_rows(out, lse):
    row, lane = iota((128, 128), 0), iota((128, 128), 1)
    diag = jnp.where(lane == (row & 15), lse, 0.0)
    high = diag.astype(BF16)
    rest = diag - high.astype(F32)
    mid = rest.astype(BF16)
    low = (rest - mid.astype(F32)).astype(BF16)
    total = jnp.where((row & 15) < 12, out, 0.0)
    for k, part in enumerate((high, mid, low)):
        place = flag(row == ((lane >> 4) * 16 + 12 + k))
        total = total + mm(place, part)
    return total


def kernel(
    node_s, len_s, slen_s, routes_s,
    q_ref, new_ref, res_ref, groot_ref, rgroup_ref, gain_ref,
    suf_hbm, kv_hbm, outw_hbm, router_hbm, wgu_hbm, wd_hbm,
    att_ref, out_ref,
    qtile, qown, qbuf, kv, feat, nl, freq, scores, ostage, oland, suf, newkv, atile, outw, router,
    pstage, pland, stream, pmat, pick, pack, xland, wgu, wd, gstage, gland, hstage, hland, rstage, rland,
    load_sem, core_send, core_recv, q_send, q_recv, o_send, o_recv, p_send, p_recv, x_send, x_recv,
    g_send, g_recv, h_send, h_recv, r_send, r_recv,
):
    x = lax.axis_index("kv")
    blk = lax.axis_index("blk")
    core = lax.rem(blk, 2)
    chip = blk // 2
    y, z = chip // NZ, lax.rem(chip, NZ)
    partner = chip * 2 + (1 - core)

    def plane_peer(c):
        return (x, c * 2 + core)

    loads = [
        pltpu.make_async_copy(kv_hbm, kv.at[pl.ds(0, KEYS)], load_sem.at[0]),
        pltpu.make_async_copy(suf_hbm, suf, load_sem.at[1]),
        pltpu.make_async_copy(outw_hbm, outw, load_sem.at[2]),
        pltpu.make_async_copy(router_hbm, router, load_sem.at[3]),
        pltpu.make_async_copy(wgu_hbm, wgu.at[0], load_sem.at[4]),
        pltpu.make_async_copy(wd_hbm, wd.at[pl.ds(0, FFP)], load_sem.at[5]),
    ]
    for copy in loads:
        copy.start()

    barrier = pltpu.get_barrier_semaphore()

    def greet(k, carry):
        pl.semaphore_signal(barrier, inc=1, device_id=plane_peer(lax.rem(chip + k, NC)), device_id_type=MESH)
        return carry

    lax.fori_loop(1, NC, greet, 0)
    pl.semaphore_signal(barrier, inc=1, device_id=(x, partner), device_id_type=MESH)
    for k in range(1, NX):
        pl.semaphore_signal(barrier, inc=1, device_id=(lax.rem(x + k, NX), blk), device_id_type=MESH)

    qtile[...] = jnp.zeros((ROWS, HD), F32)
    for h in range(HEADS):
        qtile[h * NEW:(h + 1) * NEW, :] = q_ref[:, h * HD:(h + 1) * HD].astype(F32)
    qown[...] = qtile[...].astype(BF16)

    lane8, row8 = iota((8, 128), 1), iota((8, 128), 0)
    table = jnp.where(row8 == 0, -1, 0)
    for b in range(BLOCKS):
        table = jnp.where((lane8 == b) & (row8 == 0), node_s[b], table)
        table = jnp.where((lane8 == b) & (row8 == 1), len_s[b], table)
    nl[0] = table

    pl.semaphore_wait(barrier, NC + NX - 1)

    own_q = pltpu.make_async_copy(qown, qbuf.at[y, pl.ds(z * ROWS, ROWS)], q_recv.at[y])
    own_q.start()

    def send_q(k, carry):
        peer = lax.rem(y + k // NZ, NY) * NZ + lax.rem(z + lax.rem(k, NZ), NZ)
        pltpu.make_async_remote_copy(
            src_ref=qown, dst_ref=qbuf.at[y, pl.ds(z * ROWS, ROWS)], send_sem=q_send, recv_sem=q_recv.at[y],
            device_id=plane_peer(peer), device_id_type=MESH,
        ).start()
        return carry

    lax.fori_loop(1, NC, send_q, 0)

    def to_partner(src, dst, i):
        return pltpu.make_async_remote_copy(
            src_ref=src, dst_ref=dst, send_sem=core_send.at[i], recv_sem=core_recv.at[i],
            device_id=(x, partner), device_id_type=MESH,
        )

    swaps = [
        to_partner(nl.at[0], nl.at[1], 0),
        to_partner(kv_hbm, kv.at[pl.ds(KEYS, KEYS)], 1),
        to_partner(wgu_hbm, wgu.at[1], 2),
        to_partner(wd_hbm, wd.at[pl.ds(FFP, FFP)], 3),
    ]
    for copy in swaps:
        copy.start()

    sub, lane = iota((128, 128), 0), iota((128, 128), 1)
    group_node = (jnp.where(sub == groot_ref[...], BIG, 0.0) + jnp.where(sub == lane + ROOTS, BIG, 0.0)).astype(BF16)
    in_group = flag(sub == rgroup_ref[...])
    freq[...] = mm(group_node, in_group).astype(BF16)

    esub, elane = iota((EXPERTS, 128), 0), iota((EXPERTS, 128), 1)
    seen = jnp.zeros((EXPERTS, 128), I32)
    places = [jnp.zeros((EXPERTS, 128), F32), jnp.zeros((EXPERTS, 128), F32)]
    trow, tlane = iota((8, EXPERTS), 0), iota((8, EXPERTS), 1)
    named = jnp.zeros((8, EXPERTS), I32)
    ranked = jnp.zeros((8, EXPERTS), I32)
    for t in range(NEW):
        hit = esub == routes_s[t, 0]
        row_hit = tlane == routes_s[t, 0]
        for k in range(1, TOPK):
            hit = hit | (esub == routes_s[t, k])
            row_hit = row_hit | (tlane == routes_s[t, k])
        for c in range(2):
            places[c] = jnp.where(hit & (seen == c) & ((elane & 7) == t) & (elane < 8 * GRP), 1.0, places[c])
        seen = seen + jnp.where(hit, 1, 0)
        named = named + jnp.where(row_hit & (trow == t), 1, 0)
        ranked = ranked + jnp.where(row_hit & (trow > t), 1, 0)
    prow, plane = iota((EXPERTS * ROWS, 128), 0), iota((EXPERTS * ROWS, 128), 1)
    spread = flag(iota((EXPERTS * ROWS, EXPERTS), 0) >> 4 == iota((EXPERTS * ROWS, EXPERTS), 1))
    same = (prow & 15) >> 1 == plane >> 3
    choose = jnp.where(same & ((prow & 1) == 0), mm(spread, places[0].astype(BF16)), 0.0)
    choose = jnp.where(same & ((prow & 1) == 1), mm(spread, places[1].astype(BF16)), choose)
    pick[...] = choose.astype(BF16)

    for g in range(GRP):
        s, c = iota((128, NC * ROWS), 0), iota((128, NC * ROWS), 1)
        pmat[g * 128:(g + 1) * 128, :] = flag(c == (s >> 1) * ROWS + g * 2 + (s & 1))

    loads[1].wait()
    newkv[...] = jnp.zeros((128, 2 * HD), F32)
    newkv[0:NEW, :] = new_ref[...].astype(F32)
    fresh = newkv[...].astype(BF16)
    q16 = qown[...]
    srow, slane = iota((ROWS, 128), 0), iota((ROWS, 128), 1)
    s_suffix = jnp.where(slane < slen_s[0], mmt(q16, suf[:, :HD]) * SCALE, UNSEEN)
    s_fresh = jnp.where(slane <= (srow & 3), mmt(q16, fresh[:, :HD]) * SCALE, UNSEEN)
    s_top = jnp.maximum(jnp.max(s_suffix, axis=1, keepdims=True), jnp.max(s_fresh, axis=1, keepdims=True))
    w_suffix = jnp.exp(s_suffix - s_top).astype(BF16)
    w_fresh = jnp.exp(s_fresh - s_top).astype(BF16)
    s_sum = jnp.sum(w_suffix.astype(F32), axis=1, keepdims=True) + jnp.sum(w_fresh.astype(F32), axis=1, keepdims=True)
    s_out = (mm(w_suffix, suf[:, HD:]) + mm(w_fresh, fresh[:, HD:])) / s_sum
    s_lse = jnp.broadcast_to(s_top + jnp.log(s_sum), (ROWS, HD))
    pad = jnp.zeros((128 - ROWS, HD), F32)
    own_tiles = tile_rows(jnp.concatenate([s_out, pad], axis=0), jnp.concatenate([s_lse, pad], axis=0)).astype(BF16)

    def features(part):
        node_hot = flag(sub == nl[part, 0:1, :])
        lengths = jnp.broadcast_to(nl[part, 1:2, :], (128, 128)).astype(F32).astype(BF16)
        for i in range(KEYS // SPAN):
            key, block = iota((SPAN, 128), 0) + i * SPAN, iota((SPAN, 128), 1)
            member = flag(key >> 7 == block)
            used = (key & 127).astype(F32) < mmt(member, lengths)
            feat[part * KEYS + i * SPAN:part * KEYS + (i + 1) * SPAN, :] = jnp.where(
                used, mmt(member, node_hot), 0.0
            ).astype(BF16)

    features(0)
    swaps[0].wait()
    features(1)
    loads[0].wait()
    swaps[1].wait()

    def pair(k, carry):
        ys = (lax.rem(y + NY - k, NY), lax.rem(y + k + 1, NY))
        rows = []
        for yy in ys:
            pltpu.make_async_copy(qbuf.at[yy], qbuf.at[yy], q_recv.at[yy]).wait()
            request = (yy * NZ + (sub >> 4)) * 2 + core
            nodes = mmt(flag(request == lane), freq[...]).astype(BF16)
            rows.append(jnp.concatenate([qbuf[yy], nodes], axis=1))
        query = jnp.concatenate(rows, axis=0)
        top = jnp.full((256, 128), -3e38, F32)
        for i in range(2 * KEYS // SPAN):
            span = slice(i * SPAN, (i + 1) * SPAN)
            s = mmt(query, jnp.concatenate([kv[span, :HD], feat[span, :]], axis=1))
            scores[:, span] = s
            for j in range(SPAN // 128):
                top = jnp.maximum(top, s[:, j * 128:(j + 1) * 128])
        best = jnp.max(top, axis=1, keepdims=True)
        total = jnp.zeros((256, 2 * HD), F32)
        ones = jnp.ones((SPAN, HD), BF16)
        for i in range(2 * KEYS // SPAN):
            span = slice(i * SPAN, (i + 1) * SPAN)
            weight = jnp.exp2((scores[:, span] - best) * (SCALE * LOG2E)).astype(BF16)
            total = total + mm(weight, jnp.concatenate([kv[span, HD:], ones], axis=1))
        norm = total[:, HD:]
        result = total[:, :HD] / norm
        lse = jnp.where(best > 0.5 * BIG, (best - BIG) * SCALE + jnp.log(norm), UNSEEN)
        for half, yy in enumerate(ys):
            part = slice(half * 128, (half + 1) * 128)
            ostage[yy] = tile_rows(result[part], lse[part]).astype(BF16)

            def send_o(i, carry):
                zz = lax.rem(z + i, NZ)
                pltpu.make_async_remote_copy(
                    src_ref=ostage.at[yy, pl.ds(zz * ROWS, ROWS)], dst_ref=oland.at[pl.ds(chip * ROWS, ROWS)],
                    send_sem=o_send, recv_sem=o_recv, device_id=plane_peer(yy * NZ + zz), device_id_type=MESH,
                ).start()
                return carry

            lax.fori_loop(1, NZ, send_o, 0)
            if half == 1:
                send_o(0, 0)
            else:
                @pl.when(k > 0)
                def _():
                    send_o(0, 0)

                @pl.when(k == 0)
                def _():
                    pltpu.make_async_copy(
                        ostage.at[yy, pl.ds(z * ROWS, ROWS)], oland.at[pl.ds(chip * ROWS, ROWS)], o_recv
                    ).start()
        return carry

    lax.fori_loop(0, NY // 2, pair, 0)

    pltpu.make_async_copy(oland, oland, o_recv).wait()
    tiles = jnp.concatenate([oland[...], own_tiles], axis=0)
    msrc, mcol = iota((SRC, SRC * ROWS), 0), iota((SRC, SRC * ROWS), 1)
    is_lse = (mcol >> 4 == msrc) & ((mcol & 15) >= 12) & ((mcol & 15) < 15)
    lses = jnp.where(iota((SRC, 128), 0) < NC + 1, mm(flag(is_lse), tiles), UNSEEN)
    share = jnp.exp(lses - jnp.max(lses, axis=0, keepdims=True))
    share = share / jnp.sum(share, axis=0, keepdims=True)
    share = jnp.transpose(jnp.concatenate([share, jnp.zeros((128 - SRC, 128), F32)], axis=0))[0:ROWS]
    share_high = share.astype(BF16)
    share_low = (share - share_high.astype(F32)).astype(BF16)
    shares = jnp.concatenate([share_high, share_low], axis=0)
    copies = flag(iota((128, SRC * ROWS), 1) >> 4 == iota((128, SRC * ROWS), 0))
    wide = mm(shares, copies)
    mixed = jnp.where(
        (iota((2 * ROWS, SRC * ROWS), 1) & 15) == (iota((2 * ROWS, SRC * ROWS), 0) & 15), wide, 0.0
    ).astype(BF16)
    merged = mm(mixed, tiles)
    atile[...] = merged[0:ROWS] + merged[ROWS:]
    for h in range(HEADS):
        att_ref[:, h * HD:(h + 1) * HD] = atile[h * NEW:(h + 1) * NEW, :].astype(BF16)

    loads[2].wait()
    pstage[...] = mm(att_ref[...], outw[...])
    own_p = pltpu.make_async_copy(pstage, pland.at[x], p_recv)
    own_p.start()
    for k in range(1, NX):
        pltpu.make_async_remote_copy(
            src_ref=pstage, dst_ref=pland.at[x], send_sem=p_send, recv_sem=p_recv,
            device_id=(lax.rem(x + k, NX), blk), device_id_type=MESH,
        ).start()
    stream[...] = jnp.zeros((8, D), F32)
    loads[3].wait()
    pltpu.make_async_copy(pland, pland, p_recv).wait()
    summed = pland[0] + pland[1] + pland[2] + pland[3]
    stream[0:NEW, :] = res_ref[...].astype(F32) + summed
    full = stream[...]
    inverse = lax.rsqrt(jnp.mean(full * full, axis=1, keepdims=True) + 1e-6)
    normed = full * inverse * gain_ref[...]
    quarter = pl.ds(pl.multiple_of(x * Q4, 128), Q4)
    own_stream = stream[:, quarter]
    own_normed = own_stream * inverse * gain_ref[:, quarter]

    groups = [own_normed[:, g * 128:(g + 1) * 128] for g in range(GRP)]
    packed = jnp.concatenate(groups + [jnp.zeros((128 - 8 * GRP, 128), F32)], axis=0).astype(BF16)
    pack[...] = mm(pick[...], packed).astype(BF16)
    land = pl.ds(chip * ROWS, ROWS)
    pltpu.make_async_copy(pack.at[pl.ds((chip // 2) * ROWS, ROWS)], xland.at[land], x_recv).start()

    def send_x(k, carry):
        peer = lax.rem(chip + k, NC)
        pltpu.make_async_remote_copy(
            src_ref=pack.at[pl.ds((peer // 2) * ROWS, ROWS)], dst_ref=xland.at[land], send_sem=x_send,
            recv_sem=x_recv, device_id=plane_peer(peer), device_id_type=MESH,
        ).start()
        return carry

    lax.fori_loop(1, NC, send_x, 0)

    logits = mm(normed.astype(BF16), router[...])
    gate = jnp.where(named > 0, 1.0 / (1.0 + jnp.exp(-logits)), 0.0)
    gate = gate / jnp.where(trow[:, 0:1] < NEW, jnp.sum(gate, axis=1, keepdims=True), 1.0)
    owner = flag(iota((EXPERTS, NC * ROWS), 1) >> 5 == iota((EXPERTS, NC * ROWS), 0))
    acol, arow = iota((GRP * ROWS, NC * ROWS), 1), iota((GRP * ROWS, NC * ROWS), 0)
    mixer = jnp.zeros((GRP * ROWS, NC * ROWS), F32)
    for c in range(2):
        slot_gate = jnp.where(ranked == c, gate, 0.0)
        high = slot_gate.astype(BF16).astype(F32)
        both = jnp.concatenate([high, slot_gate - high], axis=0).astype(BF16)
        spreaded = mm(jnp.concatenate([both] * GRP, axis=0), owner)
        mixer = jnp.where((acol & 15) == (arow >> 4) * 2 + c, spreaded, mixer)
    mixer = mixer.astype(BF16)

    loads[4].wait()
    swaps[2].wait()
    pltpu.make_async_copy(xland, xland, x_recv).wait()
    slots = mm(pmat[...], xland[...]).astype(BF16)
    tokens = jnp.concatenate([slots[g * 128:(g + 1) * 128] for g in range(GRP)], axis=1)
    for p in range(2):
        gstage[:, p * 2 * FFP:(p + 1) * 2 * FFP] = mm(tokens, wgu[p]).astype(BF16)
    part = SLOTS // NX
    pltpu.make_async_copy(gstage.at[pl.ds(x * part, part)], gland.at[x], g_recv).start()
    for k in range(1, NX):
        peer = lax.rem(x + k, NX)
        pltpu.make_async_remote_copy(
            src_ref=gstage.at[pl.ds(peer * part, part)], dst_ref=gland.at[x], send_sem=g_send, recv_sem=g_recv,
            device_id=(peer, blk), device_id_type=MESH,
        ).start()
    pltpu.make_async_copy(gland, gland, g_recv).wait()
    gate_up = gland[0].astype(F32) + gland[1].astype(F32) + gland[2].astype(F32) + gland[3].astype(F32)
    for p in range(2):
        gates = gate_up[:, p * 2 * FFP:p * 2 * FFP + FFP]
        ups = gate_up[:, p * 2 * FFP + FFP:(p + 1) * 2 * FFP]
        hstage[:, p * FFP:(p + 1) * FFP] = (gates / (1.0 + jnp.exp(-gates)) * ups).astype(BF16)
    mine = pl.ds(x * part, part)
    pltpu.make_async_copy(hstage, hland.at[mine], h_recv).start()
    for k in range(1, NX):
        pltpu.make_async_remote_copy(
            src_ref=hstage, dst_ref=hland.at[mine], send_sem=h_send, recv_sem=h_recv,
            device_id=(lax.rem(x + k, NX), blk), device_id_type=MESH,
        ).start()
    loads[5].wait()
    swaps[3].wait()
    pltpu.make_async_copy(hland, hland, h_recv).wait()
    down = mm(hland[...], wd[...]).astype(BF16)
    down_rows = jnp.concatenate([down[:, g * 128:(g + 1) * 128] for g in range(GRP)], axis=0)
    rstage[...] = lax.dot_general(
        pmat[...], down_rows, (((0,), (0,)), ((), ())), preferred_element_type=F32
    ).astype(BF16)
    pltpu.make_async_copy(rstage.at[land], rland.at[land], r_recv).start()

    def send_r(k, carry):
        peer = lax.rem(chip + k, NC)
        pltpu.make_async_remote_copy(
            src_ref=rstage.at[pl.ds(peer * ROWS, ROWS)], dst_ref=rland.at[land], send_sem=r_send,
            recv_sem=r_recv, device_id=plane_peer(peer), device_id_type=MESH,
        ).start()
        return carry

    lax.fori_loop(1, NC, send_r, 0)
    pltpu.make_async_copy(rland, rland, r_recv).wait()
    experts = mm(mixer, rland[...])
    for g in range(GRP):
        both = experts[g * ROWS:g * ROWS + 8] + experts[g * ROWS + 8:(g + 1) * ROWS]
        out_ref[:, g * 128:(g + 1) * 128] = (own_stream[:, g * 128:(g + 1) * 128] + both)[0:NEW].astype(BF16)

    def sent(ref, sem):
        pltpu.make_async_copy(ref, ref, sem).wait()

    many = pl.ds(0, (NC - 1) * ROWS)
    sent(oland.at[many], q_send)
    sent(oland.at[many], o_send)
    sent(oland.at[many], x_send)
    sent(oland.at[many], r_send)
    sent(pland.at[pl.ds(0, NX - 1)], p_send)
    sent(gland.at[pl.ds(0, NX - 1)], g_send)
    sent(hland.at[pl.ds(0, (NX - 1) * part)], h_send)


def local(
    residual, queries, new_kv, suffix_kv, suffix_len, shared_kv, block_node, block_len, group_root, request_group,
    out_weight, norm_gain, router, routes, expert_gate_up, expert_down,
):
    smem = pl.BlockSpec(memory_space=pltpu.SMEM)
    vmem = pl.BlockSpec(memory_space=pltpu.VMEM)
    hbm = pl.BlockSpec(memory_space=pl.ANY)
    dma = pltpu.SemaphoreType.DMA
    groups = group_root.shape[0]
    group_root = jnp.concatenate([group_root, jnp.full((128 - groups,), -1, I32)]).reshape(1, 128)
    return pl.pallas_call(
        kernel,
        out_shape=(jax.ShapeDtypeStruct((NEW, HEADS * HD), BF16), jax.ShapeDtypeStruct((NEW, Q4), BF16)),
        in_specs=[smem] * 4 + [vmem] * 6 + [hbm] * 6,
        out_specs=(vmem, vmem),
        scratch_shapes=[
            pltpu.VMEM((ROWS, HD), F32),
            pltpu.VMEM((ROWS, HD), BF16),
            pltpu.VMEM((NY, NZ * ROWS, HD), BF16),
            pltpu.VMEM((2 * KEYS, 2 * HD), BF16),
            pltpu.VMEM((2 * KEYS, 128), BF16),
            pltpu.VMEM((2, 8, 128), I32),
            pltpu.VMEM((128, 128), BF16),
            pltpu.VMEM((256, 2 * KEYS), F32),
            pltpu.VMEM((NY, NZ * ROWS, HD), BF16),
            pltpu.VMEM((NC * ROWS, HD), BF16),
            pltpu.VMEM((128, 2 * HD), BF16),
            pltpu.VMEM((128, 2 * HD), F32),
            pltpu.VMEM((ROWS, HD), F32),
            pltpu.VMEM((HEADS * HD, D), BF16),
            pltpu.VMEM((D, EXPERTS), BF16),
            pltpu.VMEM((NEW, D), F32),
            pltpu.VMEM((NX, NEW, D), F32),
            pltpu.VMEM((8, D), F32),
            pltpu.VMEM((GRP * 128, NC * ROWS), BF16),
            pltpu.VMEM((EXPERTS * ROWS, 128), BF16),
            pltpu.VMEM((EXPERTS * ROWS, 128), BF16),
            pltpu.VMEM((NC * ROWS, 128), BF16),
            pltpu.VMEM((2, Q4, 2 * FFP), BF16),
            pltpu.VMEM((2 * FFP, Q4), BF16),
            pltpu.VMEM((SLOTS, 4 * FFP), BF16),
            pltpu.VMEM((NX, SLOTS // NX, 4 * FFP), BF16),
            pltpu.VMEM((SLOTS // NX, 2 * FFP), BF16),
            pltpu.VMEM((SLOTS, 2 * FFP), BF16),
            pltpu.VMEM((NC * ROWS, 128), BF16),
            pltpu.VMEM((NC * ROWS, 128), BF16),
            dma((6,)), dma((4,)), dma((4,)), dma, dma((NY,)), dma, dma, dma, dma, dma, dma,
            dma, dma, dma, dma, dma, dma,
        ],
        compiler_params=pltpu.CompilerParams(collective_id=0, has_side_effects=True, vmem_limit_bytes=60 * 1024 * 1024),
        name="decode_step",
    )(
        block_node, block_len, suffix_len, routes,
        queries, new_kv, residual, group_root, request_group.reshape(1, 128), norm_gain.reshape(1, D),
        suffix_kv.reshape(128, 2 * HD), shared_kv.reshape(KEYS, 2 * HD), out_weight, router,
        expert_gate_up.reshape(Q4, 2 * FFP), expert_down.reshape(FFP, Q4),
    )


def solution(mesh):
    in_specs = (
        P("blk", None),
        P("blk", "kv"),
        P("blk", "kv"),
        P("blk", "kv", None, None),
        P("blk"),
        P("blk", "kv", None, None),
        P("blk"),
        P("blk"),
        P(),
        P(),
        P("kv", None),
        P(),
        P(),
        P("blk", None),
        P("blk", "kv", None),
        P("blk", None, "kv"),
    )
    out_specs = (P("blk", "kv"), P("blk", "kv"))
    return jax.shard_map(local, mesh=mesh, in_specs=in_specs, out_specs=out_specs, check_vma=False)
```

```python
import math

import jax
import jax.numpy as jnp
from jax import lax
from jax.experimental import pallas as pl
from jax.experimental.pallas import tpu as pltpu
from jax.sharding import PartitionSpec as P

MESH = pl.DeviceIdType.MESH
F32 = jnp.float32
BF16 = jnp.bfloat16
I32 = jnp.int32

HD = 128
NEW = 4
HEADS = 3
TOPK = 6
ROOTS = 16
EXPERTS = 32
NY, NZ = 8, 8
NC = NY * NZ
NX = 4
BLOCKS = 16
KEYS = BLOCKS * 128
D = 2560
Q4 = 640
FFP = 384
ROWS = 16
SLOTS = NC * 2
GRP = Q4 // 128
BIG = 16384.0
UNSEEN = -65536.0
SCALE = 1.0 / math.sqrt(HD)
LOG2E = 1.4426950408889634
SPAN = 512
PACKED = 96
PAIRS = (0, 3, 2, 1)
SRC = 72


def iota(shape, dim):
    return lax.broadcasted_iota(I32, shape, dim)


def mm(a, b):
    return jnp.dot(a, b, preferred_element_type=F32)


def mmt(a, b):
    return lax.dot_general(a, b, (((1,), (1,)), ((), ())), preferred_element_type=F32)


def flag(cond):
    return jnp.where(cond, 1.0, 0.0).astype(BF16)


def tile_rows(place, out, lse):
    row, lane = iota((PACKED, 128), 0), iota((PACKED, 128), 1)
    diag = jnp.where(lane == row - 12 * ((row * 43) >> 9), lse, 0.0)
    high = diag.astype(BF16)
    rest = diag - high.astype(F32)
    mid = rest.astype(BF16)
    low = (rest - mid.astype(F32)).astype(BF16)
    return mm(place, jnp.concatenate([out.astype(BF16), high, mid, low], axis=0)).astype(BF16)


def far_first(i):
    return 4 + (1 - 2 * lax.rem(i, 2)) * ((i + 1) // 2)


def kernel(
    node_s, len_s, slen_s, routes_s,
    q_ref, new_ref, res_ref, groot_ref, rgroup_ref, gain_ref,
    suf_hbm, kv_hbm, outw_hbm, router_hbm, wgu_hbm, wd_hbm,
    att_ref, out_ref,
    qtile, qown, qbuf, kv, feat, nl, freq, scores, ostage, oland, suf, newkv, atile, outw, router,
    place, gather, lsepick, spreads, pstage, pland, stream, pmat, pback, pick, pack, xland, wgu, wd, gstage, gland, hstage, hland, rstage, rland,
    load_sem, core_send, core_recv, q_send, q_recv, o_send, o_recv, p_send, p_recv, x_send, x_recv,
    g_send, g_recv, h_send, h_recv, r_send, r_recv,
):
    x = lax.axis_index("kv")
    blk = lax.axis_index("blk")
    core = lax.rem(blk, 2)
    chip = blk // 2
    y, z = chip // NZ, lax.rem(chip, NZ)
    partner = chip * 2 + (1 - core)

    def plane_peer(c):
        return (x, c * 2 + core)

    def far_peer(k):
        return lax.rem(y + far_first(k // NZ), NY) * NZ + lax.rem(z + far_first(lax.rem(k, NZ)), NZ)

    loads = [
        pltpu.make_async_copy(kv_hbm, kv.at[pl.ds(0, KEYS)], load_sem.at[0]),
        pltpu.make_async_copy(suf_hbm, suf, load_sem.at[1]),
        pltpu.make_async_copy(outw_hbm, outw, load_sem.at[2]),
        pltpu.make_async_copy(router_hbm, router, load_sem.at[3]),
        pltpu.make_async_copy(wgu_hbm, wgu.at[0], load_sem.at[4]),
        pltpu.make_async_copy(wd_hbm, wd.at[pl.ds(0, FFP)], load_sem.at[5]),
    ]
    for copy in loads:
        copy.start()

    barrier = pltpu.get_barrier_semaphore()

    def greet(k, carry):
        pl.semaphore_signal(barrier, inc=1, device_id=plane_peer(lax.rem(chip + k, NC)), device_id_type=MESH)
        return carry

    lax.fori_loop(1, NC, greet, 0)
    pl.semaphore_signal(barrier, inc=1, device_id=(x, partner), device_id_type=MESH)
    for k in range(1, NX):
        pl.semaphore_signal(barrier, inc=1, device_id=(lax.rem(x + k, NX), blk), device_id_type=MESH)

    qtile[...] = jnp.zeros((ROWS, HD), F32)
    for h in range(HEADS):
        qtile[h * NEW:(h + 1) * NEW, :] = q_ref[:, h * HD:(h + 1) * HD].astype(F32)
    qown[...] = qtile[...].astype(BF16)

    lane8, row8 = iota((8, 128), 1), iota((8, 128), 0)
    table = jnp.where(row8 == 0, -1, 0)
    for b in range(BLOCKS):
        table = jnp.where((lane8 == b) & (row8 == 0), node_s[b], table)
        table = jnp.where((lane8 == b) & (row8 == 1), len_s[b], table)
    nl[0] = table

    pl.semaphore_wait(barrier, NC + NX - 1)

    own_q = pltpu.make_async_copy(qown, qbuf.at[y, pl.ds(z * ROWS, ROWS)], q_recv.at[y])
    own_q.start()

    def send_q(k, carry):
        peer = lax.rem(y + k // NZ, NY) * NZ + lax.rem(z + lax.rem(k, NZ), NZ)
        pltpu.make_async_remote_copy(
            src_ref=qown, dst_ref=qbuf.at[y, pl.ds(z * ROWS, ROWS)], send_sem=q_send, recv_sem=q_recv.at[y],
            device_id=plane_peer(peer), device_id_type=MESH,
        ).start()
        return carry

    lax.fori_loop(1, NC, send_q, 0)

    def to_partner(src, dst, i):
        return pltpu.make_async_remote_copy(
            src_ref=src, dst_ref=dst, send_sem=core_send.at[i], recv_sem=core_recv.at[i],
            device_id=(x, partner), device_id_type=MESH,
        )

    swaps = [
        to_partner(nl.at[0], nl.at[1], 0),
        to_partner(kv_hbm, kv.at[pl.ds(KEYS, KEYS)], 1),
        to_partner(wgu_hbm, wgu.at[1], 2),
        to_partner(wd_hbm, wd.at[pl.ds(FFP, FFP)], 3),
    ]
    for copy in swaps:
        copy.start()

    sub, lane = iota((128, 128), 0), iota((128, 128), 1)
    groups = groot_ref.shape[1]
    node, group = iota((128, groups), 0), iota((128, groups), 1)
    group_node = jnp.where((node == groot_ref[...]) | (node == group + ROOTS), BIG, 0.0).astype(BF16)
    in_group = flag(iota((groups, 128), 0) == rgroup_ref[...])
    freq[...] = mm(group_node, in_group).astype(BF16)

    esub, elane = iota((EXPERTS, 128), 0), iota((EXPERTS, 128), 1)
    seen = jnp.zeros((EXPERTS, 128), I32)
    places = [jnp.zeros((EXPERTS, 128), F32), jnp.zeros((EXPERTS, 128), F32)]
    trow, tlane = iota((8, EXPERTS), 0), iota((8, EXPERTS), 1)
    named = jnp.zeros((8, EXPERTS), I32)
    ranked = jnp.zeros((8, EXPERTS), I32)
    for t in range(NEW):
        hit = esub == routes_s[t, 0]
        row_hit = tlane == routes_s[t, 0]
        for k in range(1, TOPK):
            hit = hit | (esub == routes_s[t, k])
            row_hit = row_hit | (tlane == routes_s[t, k])
        for c in range(2):
            places[c] = jnp.where(hit & (seen == c) & ((elane & 7) == t) & (elane < 8 * GRP), 1.0, places[c])
        seen = seen + jnp.where(hit, 1, 0)
        named = named + jnp.where(row_hit & (trow == t), 1, 0)
        ranked = ranked + jnp.where(row_hit & (trow > t), 1, 0)
    prow, plane = iota((EXPERTS * ROWS, 128), 0), iota((EXPERTS * ROWS, 128), 1)
    spread = flag(iota((EXPERTS * ROWS, EXPERTS), 0) >> 4 == iota((EXPERTS * ROWS, EXPERTS), 1))
    same = (prow & 15) >> 1 == plane >> 3
    choose = jnp.where(same & ((prow & 1) == 0), mm(spread, places[0].astype(BF16)), 0.0)
    choose = jnp.where(same & ((prow & 1) == 1), mm(spread, places[1].astype(BF16)), choose)
    pick[...] = choose.astype(BF16)

    s, c = iota((GRP * 32, 256), 0), iota((GRP * 32, 256), 1)
    pmat[...] = flag(c == ((s & 31) >> 1) * ROWS + (s >> 5) * 2 + (s & 1))
    c, s = iota((256, GRP * 32), 0), iota((256, GRP * 32), 1)
    pback[...] = flag(c == ((s & 31) >> 1) * ROWS + (s >> 5) * 2 + (s & 1))

    p, r = iota((PACKED, 128), 0), iota((PACKED, 128), 1)
    gather[...] = flag(((r & 15) < 12) & (p == (r >> 4) * 12 + (r & 15)))
    r, p = iota((128, PACKED), 0), iota((128, PACKED), 1)
    tile = (p * 43) >> 9
    place[...] = jnp.concatenate([flag(r == tile * 4 + p)] + [flag(r == tile * 16 + 12 + k) for k in range(3)], axis=1)
    msrc, mcol = iota((SRC, SRC * ROWS), 0), iota((SRC, SRC * ROWS), 1)
    lsepick[...] = flag((mcol >> 4 == msrc) & ((mcol & 15) >= 12) & ((mcol & 15) < 15))
    spreads[...] = flag(iota((128, SRC * ROWS), 1) >> 4 == iota((128, SRC * ROWS), 0))

    loads[1].wait()
    newkv[...] = jnp.zeros((128, 2 * HD), F32)
    newkv[0:NEW, :] = new_ref[...].astype(F32)
    fresh = newkv[...].astype(BF16)
    q16 = qown[...]
    srow, slane = iota((ROWS, 128), 0), iota((ROWS, 128), 1)
    s_suffix = jnp.where(slane < slen_s[0], mmt(q16, suf[:, :HD]) * SCALE, UNSEEN)
    s_fresh = jnp.where(slane <= (srow & 3), mmt(q16, fresh[:, :HD]) * SCALE, UNSEEN)
    s_top = jnp.maximum(jnp.max(s_suffix, axis=1, keepdims=True), jnp.max(s_fresh, axis=1, keepdims=True))
    w_suffix = jnp.exp(s_suffix - s_top).astype(BF16)
    w_fresh = jnp.exp(s_fresh - s_top).astype(BF16)
    s_sum = jnp.sum(w_suffix.astype(F32), axis=1, keepdims=True) + jnp.sum(w_fresh.astype(F32), axis=1, keepdims=True)
    s_out = (mm(w_suffix, suf[:, HD:]) + mm(w_fresh, fresh[:, HD:])) / s_sum
    s_lse = jnp.broadcast_to(s_top + jnp.log(s_sum), (ROWS, HD))
    pad = jnp.zeros((PACKED - ROWS, HD), F32)
    s_out, s_lse = jnp.where(srow < 12, s_out, 0.0), jnp.where(srow < 12, s_lse, 0.0)
    own_tiles = tile_rows(
        place[...], jnp.concatenate([s_out, pad], axis=0), jnp.concatenate([s_lse, pad], axis=0)
    )

    def features(part):
        node_hot = flag(sub == nl[part, 0:1, :])
        lengths = jnp.broadcast_to(nl[part, 1:2, :], (128, 128)).astype(F32).astype(BF16)
        for i in range(KEYS // SPAN):
            key, block = iota((SPAN, 128), 0) + i * SPAN, iota((SPAN, 128), 1)
            member = flag(key >> 7 == block)
            used = (key & 127).astype(F32) < mmt(member, lengths)
            feat[part * KEYS + i * SPAN:part * KEYS + (i + 1) * SPAN, :] = jnp.where(
                used, mmt(member, node_hot), 0.0
            ).astype(BF16)

    features(0)
    swaps[0].wait()
    features(1)
    loads[0].wait()
    swaps[1].wait()

    spans = [slice(i * SPAN, (i + 1) * SPAN) for i in range(2 * KEYS // SPAN)]
    pair_rows = 2 * PACKED

    def pair_ys(k):
        return (lax.rem(y + NY - k, NY), lax.rem(y + k + 1, NY))

    def pair_query(k):
        rows = []
        for yy in pair_ys(k):
            pltpu.make_async_copy(qbuf.at[yy], qbuf.at[yy], q_recv.at[yy]).wait()
            request = (yy * NZ + (sub >> 4)) * 2 + core
            nodes = mmt(flag(request == lane), freq[...]).astype(BF16)
            rows.append(mm(gather[...], jnp.concatenate([qbuf[yy], nodes], axis=1)).astype(BF16))
        return jnp.concatenate(rows, axis=0)

    def send_pair(k, best, total):
        norm = total[:, HD:]
        result = total[:, :HD] / norm
        lse = jnp.where(best > 0.5 * BIG, (best - BIG) * SCALE + jnp.log(norm), UNSEEN)
        for half, yy in enumerate(pair_ys(k)):
            rows = slice(half * PACKED, (half + 1) * PACKED)
            ostage[yy] = tile_rows(place[...], result[rows], lse[rows])

            def send_o(i, carry):
                zz = lax.rem(z + far_first(i), NZ)
                pltpu.make_async_remote_copy(
                    src_ref=ostage.at[yy, pl.ds(zz * ROWS, ROWS)], dst_ref=oland.at[pl.ds(chip * ROWS, ROWS)],
                    send_sem=o_send, recv_sem=o_recv, device_id=plane_peer(yy * NZ + zz), device_id_type=MESH,
                ).start()
                return carry

            if k == 0 and half == 0:
                lax.fori_loop(0, NZ - 1, send_o, 0)
                pltpu.make_async_copy(
                    ostage.at[yy, pl.ds(z * ROWS, ROWS)], oland.at[pl.ds(chip * ROWS, ROWS)], o_recv
                ).start()
            else:
                lax.fori_loop(0, NZ, send_o, 0)

    ones = jnp.ones((SPAN, HD), BF16)
    before = None
    for step in range(len(PAIRS) + 1):
        now = step < len(PAIRS)
        if now:
            query = pair_query(PAIRS[step])
            top = jnp.full((pair_rows, 128), -3e38, F32)
        if before is not None:
            total = jnp.zeros((pair_rows, 2 * HD), F32)
        for span in spans:
            if now:
                s = mmt(query, jnp.concatenate([kv[span, :HD], feat[span, :]], axis=1))
                scores[step % 2, :, span] = s
                for j in range(SPAN // 128):
                    top = jnp.maximum(top, s[:, j * 128:(j + 1) * 128])
            if before is not None:
                weight = jnp.exp2((scores[1 - step % 2, :, span] - before) * (SCALE * LOG2E)).astype(BF16)
                total = total + mm(weight, jnp.concatenate([kv[span, HD:], ones], axis=1))
        if before is not None:
            send_pair(PAIRS[step - 1], before, total)
        before = jnp.max(top, axis=1, keepdims=True) if now else None

    pltpu.make_async_copy(oland, oland, o_recv).wait()
    tiles = jnp.concatenate([oland[...], own_tiles], axis=0)
    lses = jnp.where(iota((SRC, 128), 0) < NC + 1, mm(lsepick[...], tiles), UNSEEN)
    share = jnp.exp(lses - jnp.max(lses, axis=0, keepdims=True))
    share = share / jnp.sum(share, axis=0, keepdims=True)
    share = jnp.transpose(jnp.concatenate([share, jnp.zeros((128 - SRC, 128), F32)], axis=0))[0:ROWS]
    share_high = share.astype(BF16)
    share_low = (share - share_high.astype(F32)).astype(BF16)
    shares = jnp.concatenate([share_high, share_low], axis=0)
    wide = mm(shares, spreads[...])
    mixed = jnp.where(
        (iota((2 * ROWS, SRC * ROWS), 1) & 15) == (iota((2 * ROWS, SRC * ROWS), 0) & 15), wide, 0.0
    ).astype(BF16)
    merged = mm(mixed, tiles)
    atile[...] = merged[0:ROWS] + merged[ROWS:]
    for h in range(HEADS):
        att_ref[:, h * HD:(h + 1) * HD] = atile[h * NEW:(h + 1) * NEW, :].astype(BF16)

    loads[2].wait()
    pstage[...] = mm(att_ref[...], outw[...]).astype(BF16)
    own_p = pltpu.make_async_copy(pstage, pland.at[x], p_recv)
    own_p.start()
    for k in range(1, NX):
        pltpu.make_async_remote_copy(
            src_ref=pstage, dst_ref=pland.at[x], send_sem=p_send, recv_sem=p_recv,
            device_id=(lax.rem(x + k, NX), blk), device_id_type=MESH,
        ).start()
    stream[...] = jnp.zeros((8, D), F32)
    loads[3].wait()
    pltpu.make_async_copy(pland, pland, p_recv).wait()
    summed = pland[0].astype(F32) + pland[1].astype(F32) + pland[2].astype(F32) + pland[3].astype(F32)
    stream[0:NEW, :] = res_ref[...].astype(F32) + summed
    full = stream[...]
    inverse = lax.rsqrt(jnp.mean(full * full, axis=1, keepdims=True) + 1e-6)
    normed = full * inverse * gain_ref[...].reshape(1, D)
    quarter = pl.ds(pl.multiple_of(x * Q4, 128), Q4)
    own_stream = stream[:, quarter]
    own_normed = own_stream * inverse * gain_ref[quarter].reshape(1, Q4)

    groups = [own_normed[:, g * 128:(g + 1) * 128] for g in range(GRP)]
    packed = jnp.concatenate(groups + [jnp.zeros((128 - 8 * GRP, 128), F32)], axis=0).astype(BF16)
    pack[...] = mm(pick[...], packed).astype(BF16)
    land = pl.ds(chip * ROWS, ROWS)
    pltpu.make_async_copy(pack.at[pl.ds((chip // 2) * ROWS, ROWS)], xland.at[land], x_recv).start()

    def send_x(k, carry):
        peer = far_peer(k)
        pltpu.make_async_remote_copy(
            src_ref=pack.at[pl.ds((peer // 2) * ROWS, ROWS)], dst_ref=xland.at[land], send_sem=x_send,
            recv_sem=x_recv, device_id=plane_peer(peer), device_id_type=MESH,
        ).start()
        return carry

    lax.fori_loop(0, NC - 1, send_x, 0)

    logits = mmt(normed.astype(BF16), router[...])
    gate = jnp.where(named > 0, 1.0 / (1.0 + jnp.exp(-logits)), 0.0)
    gate = gate / jnp.where(trow[:, 0:1] < NEW, jnp.sum(gate, axis=1, keepdims=True), 1.0)
    owner = flag(iota((EXPERTS, NC * ROWS), 1) >> 5 == iota((EXPERTS, NC * ROWS), 0))
    acol, arow = iota((GRP * ROWS, NC * ROWS), 1), iota((GRP * ROWS, NC * ROWS), 0)
    mixer = jnp.zeros((GRP * ROWS, NC * ROWS), F32)
    for c in range(2):
        slot_gate = jnp.where(ranked == c, gate, 0.0)
        high = slot_gate.astype(BF16).astype(F32)
        both = jnp.concatenate([high, slot_gate - high], axis=0).astype(BF16)
        spreaded = mm(jnp.concatenate([both] * GRP, axis=0), owner)
        mixer = jnp.where((acol & 15) == (arow >> 4) * 2 + c, spreaded, mixer)
    mixer = mixer.astype(BF16)

    loads[4].wait()
    swaps[2].wait()
    pltpu.make_async_copy(xland, xland, x_recv).wait()
    blocks = []
    for b in range(4):
        slots = mm(pmat[...], xland[b * 256:(b + 1) * 256, :]).astype(BF16)
        blocks.append(jnp.concatenate([slots[g * 32:(g + 1) * 32] for g in range(GRP)], axis=1))
    tokens = jnp.concatenate(blocks, axis=0)
    part = SLOTS // NX
    mine = pl.ds(x * part, part)
    for p in range(2):
        gstage[p] = mm(tokens, wgu[p]).astype(BF16)
        pltpu.make_async_copy(gstage.at[p, mine], gland.at[p, x], g_recv.at[p]).start()
        for k in range(1, NX):
            peer = lax.rem(x + k, NX)
            pltpu.make_async_remote_copy(
                src_ref=gstage.at[p, pl.ds(peer * part, part)], dst_ref=gland.at[p, x], send_sem=g_send.at[p],
                recv_sem=g_recv.at[p], device_id=(peer, blk), device_id_type=MESH,
            ).start()
    for p in range(2):
        pltpu.make_async_copy(gland.at[p], gland.at[p], g_recv.at[p]).wait()
        gate_up = gland[p, 0].astype(F32) + gland[p, 1].astype(F32) + gland[p, 2].astype(F32) + gland[p, 3].astype(F32)
        gates, ups = gate_up[:, :FFP], gate_up[:, FFP:]
        hstage[p] = (gates / (1.0 + jnp.exp(-gates)) * ups).astype(BF16)
        pltpu.make_async_copy(hstage.at[p], hland.at[p, mine], h_recv.at[p]).start()
        for k in range(1, NX):
            pltpu.make_async_remote_copy(
                src_ref=hstage.at[p], dst_ref=hland.at[p, mine], send_sem=h_send.at[p], recv_sem=h_recv.at[p],
                device_id=(lax.rem(x + k, NX), blk), device_id_type=MESH,
            ).start()
    loads[5].wait()
    swaps[3].wait()
    down = jnp.zeros((SLOTS, Q4), F32)
    for p in range(2):
        pltpu.make_async_copy(hland.at[p], hland.at[p], h_recv.at[p]).wait()
        down = down + mm(hland[p], wd[p * FFP:(p + 1) * FFP, :])
    down = down.astype(BF16)
    for b in range(4):
        rows = [down[b * 32:(b + 1) * 32, g * 128:(g + 1) * 128] for g in range(GRP)]
        rstage[b * 256:(b + 1) * 256, :] = mm(pback[...], jnp.concatenate(rows, axis=0)).astype(BF16)
    pltpu.make_async_copy(rstage.at[land], rland.at[land], r_recv).start()

    def send_r(k, carry):
        peer = far_peer(k)
        pltpu.make_async_remote_copy(
            src_ref=rstage.at[pl.ds(peer * ROWS, ROWS)], dst_ref=rland.at[land], send_sem=r_send,
            recv_sem=r_recv, device_id=plane_peer(peer), device_id_type=MESH,
        ).start()
        return carry

    lax.fori_loop(0, NC - 1, send_r, 0)
    pltpu.make_async_copy(rland, rland, r_recv).wait()
    experts = mm(mixer, rland[...])
    for g in range(GRP):
        both = experts[g * ROWS:g * ROWS + 8] + experts[g * ROWS + 8:(g + 1) * ROWS]
        out_ref[:, g * 128:(g + 1) * 128] = (own_stream[:, g * 128:(g + 1) * 128] + both)[0:NEW].astype(BF16)

    def sent(ref, sem):
        pltpu.make_async_copy(ref, ref, sem).wait()

    many = pl.ds(0, (NC - 1) * ROWS)
    sent(oland.at[many], q_send)
    sent(oland.at[many], o_send)
    sent(oland.at[many], x_send)
    sent(oland.at[many], r_send)
    sent(pland.at[pl.ds(0, NX - 1)], p_send)
    for p in range(2):
        sent(gland.at[p, pl.ds(0, NX - 1)], g_send.at[p])
        sent(hland.at[p, pl.ds(0, (NX - 1) * part)], h_send.at[p])


def local(
    residual, queries, new_kv, suffix_kv, suffix_len, shared_kv, block_node, block_len, group_root, request_group,
    out_weight, norm_gain, router, routes, expert_gate_up, expert_down,
):
    smem = pl.BlockSpec(memory_space=pltpu.SMEM)
    vmem = pl.BlockSpec(memory_space=pltpu.VMEM)
    hbm = pl.BlockSpec(memory_space=pl.ANY)
    dma = pltpu.SemaphoreType.DMA
    return pl.pallas_call(
        kernel,
        out_shape=(jax.ShapeDtypeStruct((NEW, HEADS * HD), BF16), jax.ShapeDtypeStruct((NEW, Q4), BF16)),
        in_specs=[smem] * 4 + [vmem] * 6 + [hbm] * 6,
        out_specs=(vmem, vmem),
        scratch_shapes=[
            pltpu.VMEM((ROWS, HD), F32),
            pltpu.VMEM((ROWS, HD), BF16),
            pltpu.VMEM((NY, NZ * ROWS, HD), BF16),
            pltpu.VMEM((2 * KEYS, 2 * HD), BF16),
            pltpu.VMEM((2 * KEYS, 128), BF16),
            pltpu.VMEM((2, 8, 128), I32),
            pltpu.VMEM((128, 128), BF16),
            pltpu.VMEM((2, 2 * PACKED, 2 * KEYS), F32),
            pltpu.VMEM((NY, NZ * ROWS, HD), BF16),
            pltpu.VMEM((NC * ROWS, HD), BF16),
            pltpu.VMEM((128, 2 * HD), BF16),
            pltpu.VMEM((128, 2 * HD), F32),
            pltpu.VMEM((ROWS, HD), F32),
            pltpu.VMEM((HEADS * HD, D), BF16),
            pltpu.VMEM((EXPERTS, D), BF16),
            pltpu.VMEM((128, 4 * PACKED), BF16),
            pltpu.VMEM((PACKED, 128), BF16),
            pltpu.VMEM((SRC, SRC * ROWS), BF16),
            pltpu.VMEM((128, SRC * ROWS), BF16),
            pltpu.VMEM((NEW, D), BF16),
            pltpu.VMEM((NX, NEW, D), BF16),
            pltpu.VMEM((8, D), F32),
            pltpu.VMEM((GRP * 32, 256), BF16),
            pltpu.VMEM((256, GRP * 32), BF16),
            pltpu.VMEM((EXPERTS * ROWS, 128), BF16),
            pltpu.VMEM((EXPERTS * ROWS, 128), BF16),
            pltpu.VMEM((NC * ROWS, 128), BF16),
            pltpu.VMEM((2, Q4, 2 * FFP), BF16),
            pltpu.VMEM((2 * FFP, Q4), BF16),
            pltpu.VMEM((2, SLOTS, 2 * FFP), BF16),
            pltpu.VMEM((2, NX, SLOTS // NX, 2 * FFP), BF16),
            pltpu.VMEM((2, SLOTS // NX, FFP), BF16),
            pltpu.VMEM((2, SLOTS, FFP), BF16),
            pltpu.VMEM((NC * ROWS, 128), BF16),
            pltpu.VMEM((NC * ROWS, 128), BF16),
            dma((6,)), dma((4,)), dma((4,)), dma, dma((NY,)), dma, dma, dma, dma, dma, dma,
            dma((2,)), dma((2,)), dma((2,)), dma((2,)), dma, dma,
        ],
        compiler_params=pltpu.CompilerParams(collective_id=0, has_side_effects=True, vmem_limit_bytes=60 * 1024 * 1024),
        name="decode_step",
    )(
        block_node, block_len, suffix_len, routes,
        queries, new_kv, residual, group_root.reshape(1, -1), request_group.reshape(1, -1), norm_gain,
        suffix_kv.reshape(128, 2 * HD), shared_kv.reshape(KEYS, 2 * HD), out_weight, router.T,
        expert_gate_up.reshape(Q4, 2 * FFP), expert_down.reshape(FFP, Q4),
    )


def solution(mesh):
    in_specs = (
        P("blk", None),
        P("blk", "kv"),
        P("blk", "kv"),
        P("blk", "kv", None, None),
        P("blk"),
        P("blk", "kv", None, None),
        P("blk"),
        P("blk"),
        P(),
        P(),
        P("kv", None),
        P(),
        P(),
        P("blk", None),
        P("blk", "kv", None),
        P("blk", None, "kv"),
    )
    out_specs = (P("blk", "kv"), P("blk", "kv"))
    return jax.shard_map(local, mesh=mesh, in_specs=in_specs, out_specs=out_specs, check_vma=False)
```

```python
import math

import jax
import jax.numpy as jnp
from jax import lax
from jax.experimental import pallas as pl
from jax.experimental.pallas import tpu as pltpu
from jax.sharding import PartitionSpec as P

MESH = pl.DeviceIdType.MESH
F32 = jnp.float32
BF16 = jnp.bfloat16
I32 = jnp.int32

HD = 128
NEW = 4
HEADS = 3
TOPK = 6
ROOTS = 16
EXPERTS = 32
NY, NZ = 8, 8
NC = NY * NZ
NX = 4
BLOCKS = 16
KEYS = BLOCKS * 128
D = 2560
Q4 = 640
FFP = 384
ROWS = 16
USED = 10
QROWS = 12
SLOTS = NC * 2
GRP = Q4 // 128
BIG = 16384.0
UNSEEN = -65536.0
SCALE = 1.0 / math.sqrt(HD)
LOG2E = 1.4426950408889634
SPAN = 512
PACKED = 96
PARTS = ((5, 4, 6, 3), (7, 2, 1, 0))
SRC = 72


def hops(offset):
    return min(offset, 8 - offset)


ORDER = sorted(
    [(dy, dz) for dy in range(NY) for dz in range(NZ) if dy or dz], key=lambda o: -hops(o[0]) - hops(o[1])
)


def iota(shape, dim):
    return lax.broadcasted_iota(I32, shape, dim)


def mm(a, b):
    return jnp.dot(a, b, preferred_element_type=F32)


def mmt(a, b):
    return lax.dot_general(a, b, (((1,), (1,)), ((), ())), preferred_element_type=F32)


def flag(cond):
    return jnp.where(cond, 1.0, 0.0).astype(BF16)


def tile_rows(place, out, lse):
    row, lane = iota((PACKED, 128), 0), iota((PACKED, 128), 1)
    diag = jnp.where(lane == row - 12 * ((row * 43) >> 9), lse, 0.0)
    high = diag.astype(BF16)
    rest = diag - high.astype(F32)
    mid = rest.astype(BF16)
    low = (rest - mid.astype(F32)).astype(BF16)
    return mm(place, jnp.concatenate([out.astype(BF16), high, mid, low], axis=0)).astype(BF16)


def kernel(
    node_s, len_s, slen_s, routes_s,
    q_ref, new_ref, res_ref, groot_ref, rgroup_ref, gain_ref,
    suf_hbm, kv_hbm, outw_hbm, router_hbm, wgu_hbm, wd_hbm,
    att_ref, out_ref,
    qtile, qown, qbuf, kv, feat, nl, freq, scores, rownode, ostage, oland, suf, newkv, atile, outw, router,
    place, gather, lsepick, spreads, pstage, pland, stream, pmat, pback, pick, pack, xland, wgu, wd, gstage, gland, hstage, hland, rstage, rland,
    load_sem, core_send, core_recv, q_send, q_recv, o_send, o_recv, p_send, p_recv, x_send, x_recv,
    g_send, g_recv, h_send, h_recv, r_send, r_recv,
):
    x = lax.axis_index("kv")
    blk = lax.axis_index("blk")
    core = lax.rem(blk, 2)
    chip = blk // 2
    y, z = chip // NZ, lax.rem(chip, NZ)
    partner = chip * 2 + (1 - core)

    def plane_peer(c):
        return (x, c * 2 + core)

    rows_y, rows_z = [lax.rem(y + o, NY) * NZ for o in range(NY)], [lax.rem(z + o, NZ) for o in range(NZ)]
    peers = [rows_y[dy] + rows_z[dz] for dy, dz in ORDER]

    loads = [
        pltpu.make_async_copy(kv_hbm, kv.at[pl.ds(0, KEYS)], load_sem.at[0]),
        pltpu.make_async_copy(suf_hbm, suf, load_sem.at[1]),
        pltpu.make_async_copy(outw_hbm, outw, load_sem.at[2]),
        pltpu.make_async_copy(router_hbm, router, load_sem.at[3]),
        pltpu.make_async_copy(wgu_hbm, wgu.at[0], load_sem.at[4]),
        pltpu.make_async_copy(wd_hbm, wd.at[pl.ds(0, FFP)], load_sem.at[5]),
    ]
    for copy in loads:
        copy.start()

    qbuf[...] = jnp.zeros_like(qbuf)
    xland[...] = jnp.zeros_like(xland)
    rland[...] = jnp.zeros_like(rland)

    barrier = pltpu.get_barrier_semaphore()

    def greet(k, carry):
        pl.semaphore_signal(barrier, inc=1, device_id=plane_peer(lax.rem(chip + k, NC)), device_id_type=MESH)
        return carry

    lax.fori_loop(1, NC, greet, 0)
    pl.semaphore_signal(barrier, inc=1, device_id=(x, partner), device_id_type=MESH)
    for k in range(1, NX):
        pl.semaphore_signal(barrier, inc=1, device_id=(lax.rem(x + k, NX), blk), device_id_type=MESH)

    qtile[...] = jnp.zeros((ROWS, HD), F32)
    for h in range(HEADS):
        qtile[h * NEW:(h + 1) * NEW, :] = q_ref[:, h * HD:(h + 1) * HD].astype(F32)
    qown[...] = qtile[...].astype(BF16)

    lane8, row8 = iota((8, 128), 1), iota((8, 128), 0)
    table = jnp.where(row8 == 0, -1, 0)
    for b in range(BLOCKS):
        table = jnp.where((lane8 == b) & (row8 == 0), node_s[b], table)
        table = jnp.where((lane8 == b) & (row8 == 1), len_s[b], table)
    nl[0] = table

    pl.semaphore_wait(barrier, NC + NX - 1)

    own_q = pltpu.make_async_copy(qown.at[pl.ds(0, QROWS)], qbuf.at[y, pl.ds(z * ROWS, QROWS)], q_recv.at[y])
    own_q.start()

    for peer in peers:
        pltpu.make_async_remote_copy(
            src_ref=qown.at[pl.ds(0, QROWS)], dst_ref=qbuf.at[y, pl.ds(z * ROWS, QROWS)], send_sem=q_send,
            recv_sem=q_recv.at[y], device_id=plane_peer(peer), device_id_type=MESH,
        ).start()

    def to_partner(src, dst, i):
        return pltpu.make_async_remote_copy(
            src_ref=src, dst_ref=dst, send_sem=core_send.at[i], recv_sem=core_recv.at[i],
            device_id=(x, partner), device_id_type=MESH,
        )

    swaps = [
        to_partner(nl.at[0], nl.at[1], 0),
        to_partner(kv_hbm, kv.at[pl.ds(KEYS, KEYS)], 1),
        to_partner(wgu_hbm, wgu.at[1], 2),
        to_partner(wd_hbm, wd.at[pl.ds(FFP, FFP)], 3),
    ]
    for copy in swaps:
        copy.start()

    sub, lane = iota((128, 128), 0), iota((128, 128), 1)
    groups = groot_ref.shape[1]
    node, group = iota((128, groups), 0), iota((128, groups), 1)
    group_node = jnp.where((node == groot_ref[...]) | (node == group + ROOTS), BIG, 0.0).astype(BF16)
    in_group = flag(iota((groups, 128), 0) == rgroup_ref[...])
    freq[...] = mm(group_node, in_group).astype(BF16)

    esub, elane = iota((EXPERTS, 128), 0), iota((EXPERTS, 128), 1)
    seen = jnp.zeros((EXPERTS, 128), I32)
    places = [jnp.zeros((EXPERTS, 128), F32), jnp.zeros((EXPERTS, 128), F32)]
    trow, tlane = iota((8, EXPERTS), 0), iota((8, EXPERTS), 1)
    named = jnp.zeros((8, EXPERTS), I32)
    ranked = jnp.zeros((8, EXPERTS), I32)
    for t in range(NEW):
        hit = esub == routes_s[t, 0]
        row_hit = tlane == routes_s[t, 0]
        for k in range(1, TOPK):
            hit = hit | (esub == routes_s[t, k])
            row_hit = row_hit | (tlane == routes_s[t, k])
        for c in range(2):
            places[c] = jnp.where(hit & (seen == c) & ((elane & 7) == t) & (elane < 8 * GRP), 1.0, places[c])
        seen = seen + jnp.where(hit, 1, 0)
        named = named + jnp.where(row_hit & (trow == t), 1, 0)
        ranked = ranked + jnp.where(row_hit & (trow > t), 1, 0)
    prow, plane = iota((EXPERTS * ROWS, 128), 0), iota((EXPERTS * ROWS, 128), 1)
    spread = flag(iota((EXPERTS * ROWS, EXPERTS), 0) >> 4 == iota((EXPERTS * ROWS, EXPERTS), 1))
    same = (prow & 15) >> 1 == plane >> 3
    choose = jnp.where(same & ((prow & 1) == 0), mm(spread, places[0].astype(BF16)), 0.0)
    choose = jnp.where(same & ((prow & 1) == 1), mm(spread, places[1].astype(BF16)), choose)
    pick[...] = choose.astype(BF16)

    s, c = iota((GRP * 32, 256), 0), iota((GRP * 32, 256), 1)
    pmat[...] = flag(c == ((s & 31) >> 1) * ROWS + (s >> 5) * 2 + (s & 1))
    c, s = iota((256, GRP * 32), 0), iota((256, GRP * 32), 1)
    pback[...] = flag(c == ((s & 31) >> 1) * ROWS + (s >> 5) * 2 + (s & 1))

    p, r = iota((PACKED, 128), 0), iota((PACKED, 128), 1)
    gather[...] = flag(((r & 15) < 12) & (p == (r >> 4) * 12 + (r & 15)))
    r, p = iota((128, PACKED), 0), iota((128, PACKED), 1)
    tile = (p * 43) >> 9
    place[...] = jnp.concatenate([flag(r == tile * 4 + p)] + [flag(r == tile * 16 + 12 + k) for k in range(3)], axis=1)
    for o in range(NY):
        request = (lax.rem(y + o, NY) * NZ + ((iota((PACKED, 128), 0) * 43) >> 9)) * 2 + core
        rownode[o] = mmt(flag(request == iota((PACKED, 128), 1)), freq[...]).astype(BF16)
    msrc, mcol = iota((SRC, SRC * ROWS), 0), iota((SRC, SRC * ROWS), 1)
    lsepick[...] = flag((mcol >> 4 == msrc) & ((mcol & 15) >= 12) & ((mcol & 15) < 15))
    spreads[...] = flag(iota((128, SRC * ROWS), 1) >> 4 == iota((128, SRC * ROWS), 0))

    loads[1].wait()
    newkv[...] = jnp.zeros((128, 2 * HD), F32)
    newkv[0:NEW, :] = new_ref[...].astype(F32)
    fresh = newkv[...].astype(BF16)
    q16 = qown[...]
    srow, slane = iota((ROWS, 128), 0), iota((ROWS, 128), 1)
    s_suffix = jnp.where(slane < slen_s[0], mmt(q16, suf[:, :HD]) * SCALE, UNSEEN)
    s_fresh = jnp.where(slane <= (srow & 3), mmt(q16, fresh[:, :HD]) * SCALE, UNSEEN)
    s_top = jnp.maximum(jnp.max(s_suffix, axis=1, keepdims=True), jnp.max(s_fresh, axis=1, keepdims=True))
    w_suffix = jnp.exp(s_suffix - s_top).astype(BF16)
    w_fresh = jnp.exp(s_fresh - s_top).astype(BF16)
    s_sum = jnp.sum(w_suffix.astype(F32), axis=1, keepdims=True) + jnp.sum(w_fresh.astype(F32), axis=1, keepdims=True)
    s_out = (mm(w_suffix, suf[:, HD:]) + mm(w_fresh, fresh[:, HD:])) / s_sum
    s_lse = jnp.broadcast_to(s_top + jnp.log(s_sum), (ROWS, HD))
    pad = jnp.zeros((PACKED - ROWS, HD), F32)
    s_out, s_lse = jnp.where(srow < 12, s_out, 0.0), jnp.where(srow < 12, s_lse, 0.0)
    own_tiles = tile_rows(
        place[...], jnp.concatenate([s_out, pad], axis=0), jnp.concatenate([s_lse, pad], axis=0)
    )

    def features(part):
        node_hot = flag(sub == nl[part, 0:1, :])
        lengths = jnp.broadcast_to(nl[part, 1:2, :], (128, 128)).astype(F32).astype(BF16)
        for i in range(KEYS // SPAN):
            key, block = iota((SPAN, 128), 0) + i * SPAN, iota((SPAN, 128), 1)
            member = flag(key >> 7 == block)
            used = (key & 127).astype(F32) < mmt(member, lengths)
            feat[part * KEYS + i * SPAN:part * KEYS + (i + 1) * SPAN, :] = jnp.where(
                used, mmt(member, node_hot), 0.0
            ).astype(BF16)

    features(0)
    swaps[0].wait()
    features(1)
    loads[0].wait()
    swaps[1].wait()

    spans = [slice(i * SPAN, (i + 1) * SPAN) for i in range(2 * KEYS // SPAN)]
    part_rows = len(PARTS[0]) * PACKED

    def part_query(offsets):
        rows = []
        for o in offsets:
            yy = lax.rem(y + o, NY)
            row = qbuf.at[yy, pl.ds(0, NZ * QROWS)]
            pltpu.make_async_copy(row, row, q_recv.at[yy]).wait()
            rows.append(jnp.concatenate([mm(gather[...], qbuf[yy]).astype(BF16), rownode[o]], axis=1))
        return jnp.concatenate(rows, axis=0)

    def send_part(offsets, best, total):
        norm = total[:, HD:]
        result = total[:, :HD] / norm
        lse = jnp.where(best > 0.5 * BIG, (best - BIG) * SCALE + jnp.log(norm), UNSEEN)
        for i, o in enumerate(offsets):
            rows = slice(i * PACKED, (i + 1) * PACKED)
            ostage[lax.rem(y + o, NY)] = tile_rows(place[...], result[rows], lse[rows])
        for dy, dz in ORDER:
            if dy in offsets:
                pltpu.make_async_remote_copy(
                    src_ref=ostage.at[lax.rem(y + dy, NY), pl.ds(lax.rem(z + dz, NZ) * ROWS, ROWS)],
                    dst_ref=oland.at[pl.ds(chip * ROWS, ROWS)], send_sem=o_send, recv_sem=o_recv,
                    device_id=plane_peer(rows_y[dy] + rows_z[dz]), device_id_type=MESH,
                ).start()
        if 0 in offsets:
            pltpu.make_async_copy(
                ostage.at[y, pl.ds(z * ROWS, ROWS)], oland.at[pl.ds(chip * ROWS, ROWS)], o_recv
            ).start()

    ones = jnp.ones((SPAN, HD), BF16)
    before = None
    for step in range(len(PARTS) + 1):
        now = step < len(PARTS)
        if now:
            query = part_query(PARTS[step])
            top = jnp.full((part_rows, 128), -3e38, F32)
        if before is not None:
            halves = [slice(0, part_rows // 2), slice(part_rows // 2, part_rows)]
            totals = [jnp.zeros((part_rows // 2, 2 * HD), F32)] * 2
        for span in spans:
            if now:
                s = mmt(query, jnp.concatenate([kv[span, :HD], feat[span, :]], axis=1))
                scores[step, :, span] = s
                for j in range(SPAN // 128):
                    top = jnp.maximum(top, s[:, j * 128:(j + 1) * 128])
            if before is not None:
                value = jnp.concatenate([kv[span, HD:], ones], axis=1)
                for i, half in enumerate(halves):
                    weight = jnp.exp2((scores[step - 1, half, span] - before[half]) * (SCALE * LOG2E)).astype(BF16)
                    totals[i] = totals[i] + mm(weight, value)
        if before is not None:
            send_part(PARTS[step - 1], before, jnp.concatenate(totals, axis=0))
        before = jnp.max(top, axis=1, keepdims=True) if now else None

    pltpu.make_async_copy(oland, oland, o_recv).wait()
    tiles = jnp.concatenate([oland[...], own_tiles], axis=0)
    lses = jnp.where(iota((SRC, 128), 0) < NC + 1, mm(lsepick[...], tiles), UNSEEN)
    share = jnp.exp(lses - jnp.max(lses, axis=0, keepdims=True))
    share = share / jnp.sum(share, axis=0, keepdims=True)
    share = jnp.transpose(jnp.concatenate([share, jnp.zeros((128 - SRC, 128), F32)], axis=0))[0:ROWS]
    share_high = share.astype(BF16)
    share_low = (share - share_high.astype(F32)).astype(BF16)
    shares = jnp.concatenate([share_high, share_low], axis=0)
    wide = mm(shares, spreads[...])
    mixed = jnp.where(
        (iota((2 * ROWS, SRC * ROWS), 1) & 15) == (iota((2 * ROWS, SRC * ROWS), 0) & 15), wide, 0.0
    ).astype(BF16)
    merged = mm(mixed, tiles)
    atile[...] = merged[0:ROWS] + merged[ROWS:]
    for h in range(HEADS):
        att_ref[:, h * HD:(h + 1) * HD] = atile[h * NEW:(h + 1) * NEW, :].astype(BF16)

    loads[2].wait()
    pstage[...] = mm(att_ref[...], outw[...]).astype(BF16)
    own_p = pltpu.make_async_copy(pstage, pland.at[x], p_recv)
    own_p.start()
    for k in range(1, NX):
        pltpu.make_async_remote_copy(
            src_ref=pstage, dst_ref=pland.at[x], send_sem=p_send, recv_sem=p_recv,
            device_id=(lax.rem(x + k, NX), blk), device_id_type=MESH,
        ).start()
    stream[...] = jnp.zeros((8, D), F32)
    loads[3].wait()
    pltpu.make_async_copy(pland, pland, p_recv).wait()
    summed = pland[0].astype(F32) + pland[1].astype(F32) + pland[2].astype(F32) + pland[3].astype(F32)
    stream[0:NEW, :] = res_ref[...].astype(F32) + summed
    full = stream[...]
    inverse = lax.rsqrt(jnp.mean(full * full, axis=1, keepdims=True) + 1e-6)
    normed = full * inverse * gain_ref[...].reshape(1, D)
    quarter = pl.ds(pl.multiple_of(x * Q4, 128), Q4)
    own_stream = stream[:, quarter]
    own_normed = own_stream * inverse * gain_ref[quarter].reshape(1, Q4)

    groups = [own_normed[:, g * 128:(g + 1) * 128] for g in range(GRP)]
    packed = jnp.concatenate(groups + [jnp.zeros((128 - 8 * GRP, 128), F32)], axis=0).astype(BF16)
    pack[...] = mm(pick[...], packed).astype(BF16)
    land = pl.ds(chip * ROWS, USED)
    pltpu.make_async_copy(pack.at[pl.ds((chip // 2) * ROWS, USED)], xland.at[land], x_recv).start()

    for peer in peers:
        pltpu.make_async_remote_copy(
            src_ref=pack.at[pl.ds((peer // 2) * ROWS, USED)], dst_ref=xland.at[land], send_sem=x_send,
            recv_sem=x_recv, device_id=plane_peer(peer), device_id_type=MESH,
        ).start()

    logits = mmt(normed.astype(BF16), router[...])
    gate = jnp.where(named > 0, 1.0 / (1.0 + jnp.exp(-logits)), 0.0)
    gate = gate / jnp.where(trow[:, 0:1] < NEW, jnp.sum(gate, axis=1, keepdims=True), 1.0)
    owner = flag(iota((EXPERTS, NC * ROWS), 1) >> 5 == iota((EXPERTS, NC * ROWS), 0))
    acol, arow = iota((GRP * ROWS, NC * ROWS), 1), iota((GRP * ROWS, NC * ROWS), 0)
    mixer = jnp.zeros((GRP * ROWS, NC * ROWS), F32)
    for c in range(2):
        slot_gate = jnp.where(ranked == c, gate, 0.0)
        high = slot_gate.astype(BF16).astype(F32)
        both = jnp.concatenate([high, slot_gate - high], axis=0).astype(BF16)
        spreaded = mm(jnp.concatenate([both] * GRP, axis=0), owner)
        mixer = jnp.where((acol & 15) == (arow >> 4) * 2 + c, spreaded, mixer)
    mixer = mixer.astype(BF16)

    loads[4].wait()
    swaps[2].wait()
    got = pl.ds(0, NC * USED)
    pltpu.make_async_copy(xland.at[got], xland.at[got], x_recv).wait()
    blocks = []
    for b in range(4):
        slots = mm(pmat[...], xland[b * 256:(b + 1) * 256, :]).astype(BF16)
        blocks.append(jnp.concatenate([slots[g * 32:(g + 1) * 32] for g in range(GRP)], axis=1))
    tokens = jnp.concatenate(blocks, axis=0)
    part = SLOTS // NX
    mine = pl.ds(x * part, part)
    for p in range(2):
        gstage[p] = mm(tokens, wgu[p]).astype(BF16)
        pltpu.make_async_copy(gstage.at[p, mine], gland.at[p, x], g_recv.at[p]).start()
        for k in range(1, NX):
            peer = lax.rem(x + k, NX)
            pltpu.make_async_remote_copy(
                src_ref=gstage.at[p, pl.ds(peer * part, part)], dst_ref=gland.at[p, x], send_sem=g_send.at[p],
                recv_sem=g_recv.at[p], device_id=(peer, blk), device_id_type=MESH,
            ).start()
    for p in range(2):
        pltpu.make_async_copy(gland.at[p], gland.at[p], g_recv.at[p]).wait()
        gate_up = gland[p, 0].astype(F32) + gland[p, 1].astype(F32) + gland[p, 2].astype(F32) + gland[p, 3].astype(F32)
        gates, ups = gate_up[:, :FFP], gate_up[:, FFP:]
        hstage[p] = (gates / (1.0 + jnp.exp(-gates)) * ups).astype(BF16)
        pltpu.make_async_copy(hstage.at[p], hland.at[p, mine], h_recv.at[p]).start()
        for k in range(1, NX):
            pltpu.make_async_remote_copy(
                src_ref=hstage.at[p], dst_ref=hland.at[p, mine], send_sem=h_send.at[p], recv_sem=h_recv.at[p],
                device_id=(lax.rem(x + k, NX), blk), device_id_type=MESH,
            ).start()
    loads[5].wait()
    swaps[3].wait()
    down = jnp.zeros((SLOTS, Q4), F32)
    for p in range(2):
        pltpu.make_async_copy(hland.at[p], hland.at[p], h_recv.at[p]).wait()
        down = down + mm(hland[p], wd[p * FFP:(p + 1) * FFP, :])
    down = down.astype(BF16)
    for b in range(4):
        rows = [down[b * 32:(b + 1) * 32, g * 128:(g + 1) * 128] for g in range(GRP)]
        rstage[b * 256:(b + 1) * 256, :] = mm(pback[...], jnp.concatenate(rows, axis=0)).astype(BF16)
    pltpu.make_async_copy(rstage.at[land], rland.at[land], r_recv).start()

    for peer in peers:
        pltpu.make_async_remote_copy(
            src_ref=rstage.at[pl.ds(peer * ROWS, USED)], dst_ref=rland.at[land], send_sem=r_send,
            recv_sem=r_recv, device_id=plane_peer(peer), device_id_type=MESH,
        ).start()
    pltpu.make_async_copy(rland.at[got], rland.at[got], r_recv).wait()
    experts = mm(mixer, rland[...])
    for g in range(GRP):
        both = experts[g * ROWS:g * ROWS + 8] + experts[g * ROWS + 8:(g + 1) * ROWS]
        out_ref[:, g * 128:(g + 1) * 128] = (own_stream[:, g * 128:(g + 1) * 128] + both)[0:NEW].astype(BF16)

    def sent(ref, sem):
        pltpu.make_async_copy(ref, ref, sem).wait()

    many = pl.ds(0, (NC - 1) * ROWS)
    sent(oland.at[pl.ds(0, (NC - 1) * QROWS)], q_send)
    sent(oland.at[many], o_send)
    few = pl.ds(0, (NC - 1) * USED)
    sent(oland.at[few], x_send)
    sent(oland.at[few], r_send)
    sent(pland.at[pl.ds(0, NX - 1)], p_send)
    for p in range(2):
        sent(gland.at[p, pl.ds(0, NX - 1)], g_send.at[p])
        sent(hland.at[p, pl.ds(0, (NX - 1) * part)], h_send.at[p])


def local(
    residual, queries, new_kv, suffix_kv, suffix_len, shared_kv, block_node, block_len, group_root, request_group,
    out_weight, norm_gain, router, routes, expert_gate_up, expert_down,
):
    smem = pl.BlockSpec(memory_space=pltpu.SMEM)
    vmem = pl.BlockSpec(memory_space=pltpu.VMEM)
    hbm = pl.BlockSpec(memory_space=pl.ANY)
    dma = pltpu.SemaphoreType.DMA
    return pl.pallas_call(
        kernel,
        out_shape=(jax.ShapeDtypeStruct((NEW, HEADS * HD), BF16), jax.ShapeDtypeStruct((NEW, Q4), BF16)),
        in_specs=[smem] * 4 + [vmem] * 6 + [hbm] * 6,
        out_specs=(vmem, vmem),
        scratch_shapes=[
            pltpu.VMEM((ROWS, HD), F32),
            pltpu.VMEM((ROWS, HD), BF16),
            pltpu.VMEM((NY, NZ * ROWS, HD), BF16),
            pltpu.VMEM((2 * KEYS, 2 * HD), BF16),
            pltpu.VMEM((2 * KEYS, 128), BF16),
            pltpu.VMEM((2, 8, 128), I32),
            pltpu.VMEM((128, 128), BF16),
            pltpu.VMEM((len(PARTS), len(PARTS[0]) * PACKED, 2 * KEYS), F32),
            pltpu.VMEM((NY, PACKED, 128), BF16),
            pltpu.VMEM((NY, NZ * ROWS, HD), BF16),
            pltpu.VMEM((NC * ROWS, HD), BF16),
            pltpu.VMEM((128, 2 * HD), BF16),
            pltpu.VMEM((128, 2 * HD), F32),
            pltpu.VMEM((ROWS, HD), F32),
            pltpu.VMEM((HEADS * HD, D), BF16),
            pltpu.VMEM((EXPERTS, D), BF16),
            pltpu.VMEM((128, 4 * PACKED), BF16),
            pltpu.VMEM((PACKED, 128), BF16),
            pltpu.VMEM((SRC, SRC * ROWS), BF16),
            pltpu.VMEM((128, SRC * ROWS), BF16),
            pltpu.VMEM((NEW, D), BF16),
            pltpu.VMEM((NX, NEW, D), BF16),
            pltpu.VMEM((8, D), F32),
            pltpu.VMEM((GRP * 32, 256), BF16),
            pltpu.VMEM((256, GRP * 32), BF16),
            pltpu.VMEM((EXPERTS * ROWS, 128), BF16),
            pltpu.VMEM((EXPERTS * ROWS, 128), BF16),
            pltpu.VMEM((NC * ROWS, 128), BF16),
            pltpu.VMEM((2, Q4, 2 * FFP), BF16),
            pltpu.VMEM((2 * FFP, Q4), BF16),
            pltpu.VMEM((2, SLOTS, 2 * FFP), BF16),
            pltpu.VMEM((2, NX, SLOTS // NX, 2 * FFP), BF16),
            pltpu.VMEM((2, SLOTS // NX, FFP), BF16),
            pltpu.VMEM((2, SLOTS, FFP), BF16),
            pltpu.VMEM((NC * ROWS, 128), BF16),
            pltpu.VMEM((NC * ROWS, 128), BF16),
            dma((6,)), dma((4,)), dma((4,)), dma, dma((NY,)), dma, dma, dma, dma, dma, dma,
            dma((2,)), dma((2,)), dma((2,)), dma((2,)), dma, dma,
        ],
        compiler_params=pltpu.CompilerParams(collective_id=0, has_side_effects=True, vmem_limit_bytes=60 * 1024 * 1024),
        name="decode_step",
    )(
        block_node, block_len, suffix_len, routes,
        queries, new_kv, residual, group_root.reshape(1, -1), request_group.reshape(1, -1), norm_gain,
        suffix_kv.reshape(128, 2 * HD), shared_kv.reshape(KEYS, 2 * HD), out_weight, router.T,
        expert_gate_up.reshape(Q4, 2 * FFP), expert_down.reshape(FFP, Q4),
    )


def solution(mesh):
    in_specs = (
        P("blk", None),
        P("blk", "kv"),
        P("blk", "kv"),
        P("blk", "kv", None, None),
        P("blk"),
        P("blk", "kv", None, None),
        P("blk"),
        P("blk"),
        P(),
        P(),
        P("kv", None),
        P(),
        P(),
        P("blk", None),
        P("blk", "kv", None),
        P("blk", None, "kv"),
    )
    out_specs = (P("blk", "kv"), P("blk", "kv"))
    return jax.shard_map(local, mesh=mesh, in_specs=in_specs, out_specs=out_specs, check_vma=False)
```

```python
import math

import jax
import jax.numpy as jnp
from jax import lax
from jax.experimental import pallas as pl
from jax.experimental.pallas import tpu as pltpu
from jax.sharding import PartitionSpec as P

MESH = pl.DeviceIdType.MESH
F32 = jnp.float32
BF16 = jnp.bfloat16
I32 = jnp.int32

HD = 128
NEW = 4
HEADS = 3
TOPK = 6
ROOTS = 16
EXPERTS = 32
NY, NZ = 8, 8
NC = NY * NZ
NX = 4
BLOCKS = 16
KEYS = BLOCKS * 128
D = 2560
Q4 = 640
FFP = 384
ROWS = 16
USED = 10
QROWS = 12
SLOTS = NC * 2
GRP = Q4 // 128
BIG = 16384.0
UNSEEN = -65536.0
SCALE = 1.0 / math.sqrt(HD)
LOG2E = 1.4426950408889634
SPAN = 512
PACKED = 96
PARTS = ((5, 4, 6, 3), (7, 2, 1, 0))
SRC = 72


def hops(offset):
    return min(offset, 8 - offset)


ORDER = sorted(
    [(dy, dz) for dy in range(NY) for dz in range(NZ) if dy or dz], key=lambda o: -hops(o[0]) - hops(o[1])
)


def iota(shape, dim):
    return lax.broadcasted_iota(I32, shape, dim)


def mm(a, b):
    return jnp.dot(a, b, preferred_element_type=F32)


def mmt(a, b):
    return lax.dot_general(a, b, (((1,), (1,)), ((), ())), preferred_element_type=F32)


def flag(cond):
    return jnp.where(cond, 1.0, 0.0).astype(BF16)


def tile_rows(place, out, lse):
    row, lane = iota((PACKED, 128), 0), iota((PACKED, 128), 1)
    diag = jnp.where(lane == row - 12 * ((row * 43) >> 9), lse, 0.0)
    high = diag.astype(BF16)
    rest = diag - high.astype(F32)
    mid = rest.astype(BF16)
    low = (rest - mid.astype(F32)).astype(BF16)
    return mm(place, jnp.concatenate([out.astype(BF16), high, mid, low], axis=0)).astype(BF16)


def kernel(
    node_hbm, len_hbm, slen_hbm, routes_hbm,
    q_hbm, new_hbm, res_hbm, groot_hbm, rgroup_hbm, gain_hbm,
    suf_hbm, kv_hbm, outw_hbm, router_hbm, wgu_hbm, wd_hbm,
    att_ref, out_ref,
    node_s, len_s, slen_s, routes_s, q_ref, new_ref, res_ref, groot_ref, rgroup_ref, gain_ref,
    qtile, qown, qbuf, kv, feat, nl, freq, scores, rownode, ostage, oland, suf, newkv, atile, outw, router,
    place, gather, lsepick, spreads, pstage, pland, stream, pmat, pback, pick, pack, xland, wgu, wd, gstage, gland, hstage, hland, rstage, rland,
    small_sem, load_sem, core_send, core_recv, q_send, q_recv, o_send, o_recv, p_send, p_recv, x_send, x_recv,
    g_send, g_recv, h_send, h_recv, r_send, r_recv,
):
    x = lax.axis_index("kv")
    blk = lax.axis_index("blk")
    core = lax.rem(blk, 2)
    chip = blk // 2
    y, z = chip // NZ, lax.rem(chip, NZ)
    partner = chip * 2 + (1 - core)

    def plane_peer(c):
        return (x, c * 2 + core)

    rows_y, rows_z = [lax.rem(y + o, NY) * NZ for o in range(NY)], [lax.rem(z + o, NZ) for o in range(NZ)]
    peers = [rows_y[dy] + rows_z[dz] for dy, dz in ORDER]

    smalls = [
        pltpu.make_async_copy(src, dst, small_sem.at[i])
        for i, (src, dst) in enumerate((
            (q_hbm, q_ref), (node_hbm, node_s), (len_hbm, len_s), (groot_hbm, groot_ref), (rgroup_hbm, rgroup_ref),
            (routes_hbm, routes_s), (slen_hbm, slen_s), (new_hbm, new_ref), (res_hbm, res_ref), (gain_hbm, gain_ref),
        ))
    ]
    for copy in smalls:
        copy.start()
    loads = [
        pltpu.make_async_copy(kv_hbm, kv.at[pl.ds(0, KEYS)], load_sem.at[0]),
        pltpu.make_async_copy(suf_hbm, suf, load_sem.at[1]),
        pltpu.make_async_copy(outw_hbm, outw, load_sem.at[2]),
        pltpu.make_async_copy(router_hbm, router, load_sem.at[3]),
        pltpu.make_async_copy(wgu_hbm, wgu.at[0], load_sem.at[4]),
        pltpu.make_async_copy(wd_hbm, wd.at[pl.ds(0, FFP)], load_sem.at[5]),
    ]
    for copy in loads:
        copy.start()

    qbuf[...] = jnp.zeros_like(qbuf)
    xland[...] = jnp.zeros_like(xland)
    rland[...] = jnp.zeros_like(rland)

    barrier = pltpu.get_barrier_semaphore()

    for peer in peers:
        pl.semaphore_signal(barrier, inc=1, device_id=plane_peer(peer), device_id_type=MESH)
    pl.semaphore_signal(barrier, inc=1, device_id=(x, partner), device_id_type=MESH)
    for k in range(1, NX):
        pl.semaphore_signal(barrier, inc=1, device_id=(lax.rem(x + k, NX), blk), device_id_type=MESH)

    for copy in smalls:
        copy.wait()
    qtile[...] = jnp.zeros((ROWS, HD), F32)
    for h in range(HEADS):
        qtile[h * NEW:(h + 1) * NEW, :] = q_ref[:, h * HD:(h + 1) * HD].astype(F32)
    qown[...] = qtile[...].astype(BF16)

    lane8, row8 = iota((8, 128), 1), iota((8, 128), 0)
    table = jnp.where(row8 == 0, -1, 0)
    for b in range(BLOCKS):
        table = jnp.where((lane8 == b) & (row8 == 0), node_s[b], table)
        table = jnp.where((lane8 == b) & (row8 == 1), len_s[b], table)
    nl[0] = table

    pl.semaphore_wait(barrier, NC + NX - 1)

    own_q = pltpu.make_async_copy(qown.at[pl.ds(0, QROWS)], qbuf.at[y, pl.ds(z * ROWS, QROWS)], q_recv.at[y])
    own_q.start()

    for peer in peers:
        pltpu.make_async_remote_copy(
            src_ref=qown.at[pl.ds(0, QROWS)], dst_ref=qbuf.at[y, pl.ds(z * ROWS, QROWS)], send_sem=q_send,
            recv_sem=q_recv.at[y], device_id=plane_peer(peer), device_id_type=MESH,
        ).start()

    def to_partner(src, dst, i):
        return pltpu.make_async_remote_copy(
            src_ref=src, dst_ref=dst, send_sem=core_send.at[i], recv_sem=core_recv.at[i],
            device_id=(x, partner), device_id_type=MESH,
        )

    swaps = [
        to_partner(nl.at[0], nl.at[1], 0),
        to_partner(kv_hbm, kv.at[pl.ds(KEYS, KEYS)], 1),
        to_partner(wgu_hbm, wgu.at[1], 2),
        to_partner(wd_hbm, wd.at[pl.ds(FFP, FFP)], 3),
    ]
    for copy in swaps:
        copy.start()

    sub, lane = iota((128, 128), 0), iota((128, 128), 1)
    groups = groot_ref.shape[1]
    node, group = iota((128, groups), 0), iota((128, groups), 1)
    group_node = jnp.where((node == groot_ref[...]) | (node == group + ROOTS), BIG, 0.0).astype(BF16)
    in_group = flag(iota((groups, 128), 0) == rgroup_ref[...])
    freq[...] = mm(group_node, in_group).astype(BF16)

    esub, elane = iota((EXPERTS, 128), 0), iota((EXPERTS, 128), 1)
    seen = jnp.zeros((EXPERTS, 128), I32)
    places = [jnp.zeros((EXPERTS, 128), F32), jnp.zeros((EXPERTS, 128), F32)]
    trow, tlane = iota((8, EXPERTS), 0), iota((8, EXPERTS), 1)
    named = jnp.zeros((8, EXPERTS), I32)
    ranked = jnp.zeros((8, EXPERTS), I32)
    for t in range(NEW):
        hit = esub == routes_s[t, 0]
        row_hit = tlane == routes_s[t, 0]
        for k in range(1, TOPK):
            hit = hit | (esub == routes_s[t, k])
            row_hit = row_hit | (tlane == routes_s[t, k])
        for c in range(2):
            places[c] = jnp.where(hit & (seen == c) & ((elane & 7) == t) & (elane < 8 * GRP), 1.0, places[c])
        seen = seen + jnp.where(hit, 1, 0)
        named = named + jnp.where(row_hit & (trow == t), 1, 0)
        ranked = ranked + jnp.where(row_hit & (trow > t), 1, 0)
    prow, plane = iota((EXPERTS * ROWS, 128), 0), iota((EXPERTS * ROWS, 128), 1)
    spread = flag(iota((EXPERTS * ROWS, EXPERTS), 0) >> 4 == iota((EXPERTS * ROWS, EXPERTS), 1))
    same = (prow & 15) >> 1 == plane >> 3
    choose = jnp.where(same & ((prow & 1) == 0), mm(spread, places[0].astype(BF16)), 0.0)
    choose = jnp.where(same & ((prow & 1) == 1), mm(spread, places[1].astype(BF16)), choose)
    pick[...] = choose.astype(BF16)

    s, c = iota((GRP * 32, 256), 0), iota((GRP * 32, 256), 1)
    pmat[...] = flag(c == ((s & 31) >> 1) * ROWS + (s >> 5) * 2 + (s & 1))
    c, s = iota((256, GRP * 32), 0), iota((256, GRP * 32), 1)
    pback[...] = flag(c == ((s & 31) >> 1) * ROWS + (s >> 5) * 2 + (s & 1))

    p, r = iota((PACKED, 128), 0), iota((PACKED, 128), 1)
    gather[...] = flag(((r & 15) < 12) & (p == (r >> 4) * 12 + (r & 15)))
    r, p = iota((128, PACKED), 0), iota((128, PACKED), 1)
    tile = (p * 43) >> 9
    place[...] = jnp.concatenate([flag(r == tile * 4 + p)] + [flag(r == tile * 16 + 12 + k) for k in range(3)], axis=1)
    for o in range(NY):
        request = (lax.rem(y + o, NY) * NZ + ((iota((PACKED, 128), 0) * 43) >> 9)) * 2 + core
        rownode[o] = mmt(flag(request == iota((PACKED, 128), 1)), freq[...]).astype(BF16)
    msrc, mcol = iota((SRC, SRC * ROWS), 0), iota((SRC, SRC * ROWS), 1)
    lsepick[...] = flag((mcol >> 4 == msrc) & ((mcol & 15) >= 12) & ((mcol & 15) < 15))
    spreads[...] = flag(iota((128, SRC * ROWS), 1) >> 4 == iota((128, SRC * ROWS), 0))

    loads[1].wait()
    newkv[...] = jnp.zeros((128, 2 * HD), F32)
    newkv[0:NEW, :] = new_ref[...].astype(F32)
    fresh = newkv[...].astype(BF16)
    q16 = qown[...]
    srow, slane = iota((ROWS, 128), 0), iota((ROWS, 128), 1)
    s_suffix = jnp.where(slane < slen_s[0], mmt(q16, suf[:, :HD]) * SCALE, UNSEEN)
    s_fresh = jnp.where(slane <= (srow & 3), mmt(q16, fresh[:, :HD]) * SCALE, UNSEEN)
    s_top = jnp.maximum(jnp.max(s_suffix, axis=1, keepdims=True), jnp.max(s_fresh, axis=1, keepdims=True))
    w_suffix = jnp.exp(s_suffix - s_top).astype(BF16)
    w_fresh = jnp.exp(s_fresh - s_top).astype(BF16)
    s_sum = jnp.sum(w_suffix.astype(F32), axis=1, keepdims=True) + jnp.sum(w_fresh.astype(F32), axis=1, keepdims=True)
    s_out = (mm(w_suffix, suf[:, HD:]) + mm(w_fresh, fresh[:, HD:])) / s_sum
    s_lse = jnp.broadcast_to(s_top + jnp.log(s_sum), (ROWS, HD))
    pad = jnp.zeros((PACKED - ROWS, HD), F32)
    s_out, s_lse = jnp.where(srow < 12, s_out, 0.0), jnp.where(srow < 12, s_lse, 0.0)
    own_tiles = tile_rows(
        place[...], jnp.concatenate([s_out, pad], axis=0), jnp.concatenate([s_lse, pad], axis=0)
    )

    def features(part):
        node_hot = flag(sub == nl[part, 0:1, :])
        lengths = jnp.broadcast_to(nl[part, 1:2, :], (128, 128)).astype(F32).astype(BF16)
        for i in range(KEYS // SPAN):
            key, block = iota((SPAN, 128), 0) + i * SPAN, iota((SPAN, 128), 1)
            member = flag(key >> 7 == block)
            used = (key & 127).astype(F32) < mmt(member, lengths)
            feat[part * KEYS + i * SPAN:part * KEYS + (i + 1) * SPAN, :] = jnp.where(
                used, mmt(member, node_hot), 0.0
            ).astype(BF16)

    features(0)
    swaps[0].wait()
    features(1)
    loads[0].wait()
    swaps[1].wait()

    spans = [slice(i * SPAN, (i + 1) * SPAN) for i in range(2 * KEYS // SPAN)]
    part_rows = len(PARTS[0]) * PACKED

    def part_query(offsets):
        rows = []
        for o in offsets:
            yy = lax.rem(y + o, NY)
            row = qbuf.at[yy, pl.ds(0, NZ * QROWS)]
            pltpu.make_async_copy(row, row, q_recv.at[yy]).wait()
            rows.append(jnp.concatenate([mm(gather[...], qbuf[yy]).astype(BF16), rownode[o]], axis=1))
        return jnp.concatenate(rows, axis=0)

    def send_part(offsets, best, total):
        norm = total[:, HD:]
        result = total[:, :HD] / norm
        lse = jnp.where(best > 0.5 * BIG, (best - BIG) * SCALE + jnp.log(norm), UNSEEN)
        for i, o in enumerate(offsets):
            rows = slice(i * PACKED, (i + 1) * PACKED)
            ostage[lax.rem(y + o, NY)] = tile_rows(place[...], result[rows], lse[rows])
        for dy, dz in ORDER:
            if dy in offsets:
                pltpu.make_async_remote_copy(
                    src_ref=ostage.at[lax.rem(y + dy, NY), pl.ds(lax.rem(z + dz, NZ) * ROWS, ROWS)],
                    dst_ref=oland.at[pl.ds(chip * ROWS, ROWS)], send_sem=o_send, recv_sem=o_recv,
                    device_id=plane_peer(rows_y[dy] + rows_z[dz]), device_id_type=MESH,
                ).start()
        if 0 in offsets:
            pltpu.make_async_copy(
                ostage.at[y, pl.ds(z * ROWS, ROWS)], oland.at[pl.ds(chip * ROWS, ROWS)], o_recv
            ).start()

    ones = jnp.ones((SPAN, HD), BF16)
    before = None
    for step in range(len(PARTS) + 1):
        now = step < len(PARTS)
        if now:
            query = part_query(PARTS[step])
            top = jnp.full((part_rows, 128), -3e38, F32)
        if before is not None:
            halves = [slice(0, part_rows // 2), slice(part_rows // 2, part_rows)]
            totals = [jnp.zeros((part_rows // 2, 2 * HD), F32)] * 2
        for span in spans:
            if now:
                s = mmt(query, jnp.concatenate([kv[span, :HD], feat[span, :]], axis=1))
                scores[step, :, span] = s
                for j in range(SPAN // 128):
                    top = jnp.maximum(top, s[:, j * 128:(j + 1) * 128])
            if before is not None:
                value = jnp.concatenate([kv[span, HD:], ones], axis=1)
                for i, half in enumerate(halves):
                    weight = jnp.exp2((scores[step - 1, half, span] - before[half]) * (SCALE * LOG2E)).astype(BF16)
                    totals[i] = totals[i] + mm(weight, value)
        if before is not None:
            send_part(PARTS[step - 1], before, jnp.concatenate(totals, axis=0))
        before = jnp.max(top, axis=1, keepdims=True) if now else None

    pltpu.make_async_copy(oland, oland, o_recv).wait()
    tiles = jnp.concatenate([oland[...], own_tiles], axis=0)
    lses = jnp.where(iota((SRC, 128), 0) < NC + 1, mm(lsepick[...], tiles), UNSEEN)
    share = jnp.exp(lses - jnp.max(lses, axis=0, keepdims=True))
    share = share / jnp.sum(share, axis=0, keepdims=True)
    share = jnp.transpose(jnp.concatenate([share, jnp.zeros((128 - SRC, 128), F32)], axis=0))[0:ROWS]
    share_high = share.astype(BF16)
    share_low = (share - share_high.astype(F32)).astype(BF16)
    shares = jnp.concatenate([share_high, share_low], axis=0)
    wide = mm(shares, spreads[...])
    mixed = jnp.where(
        (iota((2 * ROWS, SRC * ROWS), 1) & 15) == (iota((2 * ROWS, SRC * ROWS), 0) & 15), wide, 0.0
    ).astype(BF16)
    merged = mm(mixed, tiles)
    atile[...] = merged[0:ROWS] + merged[ROWS:]
    for h in range(HEADS):
        att_ref[:, h * HD:(h + 1) * HD] = atile[h * NEW:(h + 1) * NEW, :].astype(BF16)

    loads[2].wait()
    pstage[...] = mm(att_ref[...], outw[...]).astype(BF16)
    own_p = pltpu.make_async_copy(pstage, pland.at[x], p_recv)
    own_p.start()
    for k in (2, 1, 3):
        pltpu.make_async_remote_copy(
            src_ref=pstage, dst_ref=pland.at[x], send_sem=p_send, recv_sem=p_recv,
            device_id=(lax.rem(x + k, NX), blk), device_id_type=MESH,
        ).start()
    stream[...] = jnp.zeros((8, D), F32)
    loads[3].wait()
    pltpu.make_async_copy(pland, pland, p_recv).wait()
    summed = pland[0].astype(F32) + pland[1].astype(F32) + pland[2].astype(F32) + pland[3].astype(F32)
    stream[0:NEW, :] = res_ref[...].astype(F32) + summed
    full = stream[...]
    inverse = lax.rsqrt(jnp.mean(full * full, axis=1, keepdims=True) + 1e-6)
    normed = full * inverse * gain_ref[...].reshape(1, D)
    quarter = pl.ds(pl.multiple_of(x * Q4, 128), Q4)
    own_stream = stream[:, quarter]
    own_normed = own_stream * inverse * gain_ref[quarter].reshape(1, Q4)

    groups = [own_normed[:, g * 128:(g + 1) * 128] for g in range(GRP)]
    packed = jnp.concatenate(groups + [jnp.zeros((128 - 8 * GRP, 128), F32)], axis=0).astype(BF16)
    pack[...] = mm(pick[...], packed).astype(BF16)
    land = pl.ds(chip * ROWS, USED)
    pltpu.make_async_copy(pack.at[pl.ds((chip // 2) * ROWS, USED)], xland.at[land], x_recv).start()

    for peer in peers:
        pltpu.make_async_remote_copy(
            src_ref=pack.at[pl.ds((peer // 2) * ROWS, USED)], dst_ref=xland.at[land], send_sem=x_send,
            recv_sem=x_recv, device_id=plane_peer(peer), device_id_type=MESH,
        ).start()

    logits = mmt(normed.astype(BF16), router[...])
    gate = jnp.where(named > 0, 1.0 / (1.0 + jnp.exp(-logits)), 0.0)
    gate = gate / jnp.where(trow[:, 0:1] < NEW, jnp.sum(gate, axis=1, keepdims=True), 1.0)
    owner = flag(iota((EXPERTS, NC * ROWS), 1) >> 5 == iota((EXPERTS, NC * ROWS), 0))
    acol, arow = iota((GRP * ROWS, NC * ROWS), 1), iota((GRP * ROWS, NC * ROWS), 0)
    mixer = jnp.zeros((GRP * ROWS, NC * ROWS), F32)
    for c in range(2):
        slot_gate = jnp.where(ranked == c, gate, 0.0)
        high = slot_gate.astype(BF16).astype(F32)
        both = jnp.concatenate([high, slot_gate - high], axis=0).astype(BF16)
        spreaded = mm(jnp.concatenate([both] * GRP, axis=0), owner)
        mixer = jnp.where((acol & 15) == (arow >> 4) * 2 + c, spreaded, mixer)
    mixer = mixer.astype(BF16)

    loads[4].wait()
    swaps[2].wait()
    got = pl.ds(0, NC * USED)
    pltpu.make_async_copy(xland.at[got], xland.at[got], x_recv).wait()
    blocks = []
    for b in range(4):
        slots = mm(pmat[...], xland[b * 256:(b + 1) * 256, :]).astype(BF16)
        blocks.append(jnp.concatenate([slots[g * 32:(g + 1) * 32] for g in range(GRP)], axis=1))
    tokens = jnp.concatenate(blocks, axis=0)
    part = SLOTS // NX
    mine = pl.ds(x * part, part)
    for p in range(2):
        gstage[p] = mm(tokens, wgu[p]).astype(BF16)
        pltpu.make_async_copy(gstage.at[p, mine], gland.at[p, x], g_recv.at[p]).start()
        for k in (2, 1, 3):
            peer = lax.rem(x + k, NX)
            pltpu.make_async_remote_copy(
                src_ref=gstage.at[p, pl.ds(peer * part, part)], dst_ref=gland.at[p, x], send_sem=g_send.at[p],
                recv_sem=g_recv.at[p], device_id=(peer, blk), device_id_type=MESH,
            ).start()
    for p in range(2):
        pltpu.make_async_copy(gland.at[p], gland.at[p], g_recv.at[p]).wait()
        gate_up = gland[p, 0].astype(F32) + gland[p, 1].astype(F32) + gland[p, 2].astype(F32) + gland[p, 3].astype(F32)
        gates, ups = gate_up[:, :FFP], gate_up[:, FFP:]
        hstage[p] = (gates / (1.0 + jnp.exp(-gates)) * ups).astype(BF16)
        pltpu.make_async_copy(hstage.at[p], hland.at[p, mine], h_recv.at[p]).start()
        for k in (2, 1, 3):
            pltpu.make_async_remote_copy(
                src_ref=hstage.at[p], dst_ref=hland.at[p, mine], send_sem=h_send.at[p], recv_sem=h_recv.at[p],
                device_id=(lax.rem(x + k, NX), blk), device_id_type=MESH,
            ).start()
    loads[5].wait()
    swaps[3].wait()
    down = jnp.zeros((SLOTS, Q4), F32)
    for p in range(2):
        pltpu.make_async_copy(hland.at[p], hland.at[p], h_recv.at[p]).wait()
        down = down + mm(hland[p], wd[p * FFP:(p + 1) * FFP, :])
    down = down.astype(BF16)
    for b in range(4):
        rows = [down[b * 32:(b + 1) * 32, g * 128:(g + 1) * 128] for g in range(GRP)]
        rstage[b * 256:(b + 1) * 256, :] = mm(pback[...], jnp.concatenate(rows, axis=0)).astype(BF16)
    pltpu.make_async_copy(rstage.at[land], rland.at[land], r_recv).start()

    for peer in peers:
        pltpu.make_async_remote_copy(
            src_ref=rstage.at[pl.ds(peer * ROWS, USED)], dst_ref=rland.at[land], send_sem=r_send,
            recv_sem=r_recv, device_id=plane_peer(peer), device_id_type=MESH,
        ).start()
    pltpu.make_async_copy(rland.at[got], rland.at[got], r_recv).wait()
    experts = mm(mixer, rland[...])
    for g in range(GRP):
        both = experts[g * ROWS:g * ROWS + 8] + experts[g * ROWS + 8:(g + 1) * ROWS]
        out_ref[:, g * 128:(g + 1) * 128] = (own_stream[:, g * 128:(g + 1) * 128] + both)[0:NEW].astype(BF16)

    def sent(ref, sem):
        pltpu.make_async_copy(ref, ref, sem).wait()

    many = pl.ds(0, (NC - 1) * ROWS)
    sent(oland.at[pl.ds(0, (NC - 1) * QROWS)], q_send)
    sent(oland.at[many], o_send)
    few = pl.ds(0, (NC - 1) * USED)
    sent(oland.at[few], x_send)
    sent(oland.at[few], r_send)
    sent(pland.at[pl.ds(0, NX - 1)], p_send)
    for p in range(2):
        sent(gland.at[p, pl.ds(0, NX - 1)], g_send.at[p])
        sent(hland.at[p, pl.ds(0, (NX - 1) * part)], h_send.at[p])


def hand_on(att_ref, out_ref, att_out, layer_out):
    att_out[...] = att_ref[...]
    layer_out[...] = out_ref[...]


def local(
    residual, queries, new_kv, suffix_kv, suffix_len, shared_kv, block_node, block_len, group_root, request_group,
    out_weight, norm_gain, router, routes, expert_gate_up, expert_down,
):
    vmem = pl.BlockSpec(memory_space=pltpu.VMEM)
    hbm = pl.BlockSpec(memory_space=pl.ANY)
    dma = pltpu.SemaphoreType.DMA
    results = pl.pallas_call(
        kernel,
        out_shape=(jax.ShapeDtypeStruct((NEW, HEADS * HD), BF16), jax.ShapeDtypeStruct((NEW, Q4), BF16)),
        in_specs=[hbm] * 16,
        out_specs=(vmem, vmem),
        scratch_shapes=[
            pltpu.SMEM(block_node.shape, I32),
            pltpu.SMEM(block_len.shape, I32),
            pltpu.SMEM(suffix_len.shape, I32),
            pltpu.SMEM(routes.shape, I32),
            pltpu.VMEM(queries.shape, BF16),
            pltpu.VMEM(new_kv.shape, BF16),
            pltpu.VMEM(residual.shape, BF16),
            pltpu.VMEM((1, group_root.shape[0]), I32),
            pltpu.VMEM((1, 128), I32),
            pltpu.VMEM((D,), F32),
            pltpu.VMEM((ROWS, HD), F32),
            pltpu.VMEM((ROWS, HD), BF16),
            pltpu.VMEM((NY, NZ * ROWS, HD), BF16),
            pltpu.VMEM((2 * KEYS, 2 * HD), BF16),
            pltpu.VMEM((2 * KEYS, 128), BF16),
            pltpu.VMEM((2, 8, 128), I32),
            pltpu.VMEM((128, 128), BF16),
            pltpu.VMEM((len(PARTS), len(PARTS[0]) * PACKED, 2 * KEYS), F32),
            pltpu.VMEM((NY, PACKED, 128), BF16),
            pltpu.VMEM((NY, NZ * ROWS, HD), BF16),
            pltpu.VMEM((NC * ROWS, HD), BF16),
            pltpu.VMEM((128, 2 * HD), BF16),
            pltpu.VMEM((128, 2 * HD), F32),
            pltpu.VMEM((ROWS, HD), F32),
            pltpu.VMEM((HEADS * HD, D), BF16),
            pltpu.VMEM((EXPERTS, D), BF16),
            pltpu.VMEM((128, 4 * PACKED), BF16),
            pltpu.VMEM((PACKED, 128), BF16),
            pltpu.VMEM((SRC, SRC * ROWS), BF16),
            pltpu.VMEM((128, SRC * ROWS), BF16),
            pltpu.VMEM((NEW, D), BF16),
            pltpu.VMEM((NX, NEW, D), BF16),
            pltpu.VMEM((8, D), F32),
            pltpu.VMEM((GRP * 32, 256), BF16),
            pltpu.VMEM((256, GRP * 32), BF16),
            pltpu.VMEM((EXPERTS * ROWS, 128), BF16),
            pltpu.VMEM((EXPERTS * ROWS, 128), BF16),
            pltpu.VMEM((NC * ROWS, 128), BF16),
            pltpu.VMEM((2, Q4, 2 * FFP), BF16),
            pltpu.VMEM((2 * FFP, Q4), BF16),
            pltpu.VMEM((2, SLOTS, 2 * FFP), BF16),
            pltpu.VMEM((2, NX, SLOTS // NX, 2 * FFP), BF16),
            pltpu.VMEM((2, SLOTS // NX, FFP), BF16),
            pltpu.VMEM((2, SLOTS, FFP), BF16),
            pltpu.VMEM((NC * ROWS, 128), BF16),
            pltpu.VMEM((NC * ROWS, 128), BF16),
            dma((10,)), dma((6,)), dma((4,)), dma((4,)), dma, dma((NY,)), dma, dma, dma, dma, dma, dma,
            dma((2,)), dma((2,)), dma((2,)), dma((2,)), dma, dma,
        ],
        compiler_params=pltpu.CompilerParams(collective_id=0, has_side_effects=True, vmem_limit_bytes=60 * 1024 * 1024),
        name="decode_step",
    )(
        block_node, block_len, suffix_len, routes,
        queries, new_kv, residual, group_root.reshape(1, -1), request_group.reshape(1, -1), norm_gain,
        suffix_kv.reshape(128, 2 * HD), shared_kv.reshape(KEYS, 2 * HD), out_weight, router.T,
        expert_gate_up.reshape(Q4, 2 * FFP), expert_down.reshape(FFP, Q4),
    )
    return pl.pallas_call(
        hand_on,
        out_shape=(jax.ShapeDtypeStruct((NEW, HEADS * HD), BF16), jax.ShapeDtypeStruct((NEW, Q4), BF16)),
        in_specs=[vmem] * 2,
        out_specs=(vmem, vmem),
        name="hand_on",
    )(*results)


def solution(mesh):
    in_specs = (
        P("blk", None),
        P("blk", "kv"),
        P("blk", "kv"),
        P("blk", "kv", None, None),
        P("blk"),
        P("blk", "kv", None, None),
        P("blk"),
        P("blk"),
        P(),
        P(),
        P("kv", None),
        P(),
        P(),
        P("blk", None),
        P("blk", "kv", None),
        P("blk", None, "kv"),
    )
    out_specs = (P("blk", "kv"), P("blk", "kv"))
    return jax.shard_map(local, mesh=mesh, in_specs=in_specs, out_specs=out_specs, check_vma=False)
```

```python
import math

import jax
import jax.numpy as jnp
from jax import lax
from jax.experimental import pallas as pl
from jax.experimental.pallas import tpu as pltpu
from jax.sharding import PartitionSpec as P

MESH = pl.DeviceIdType.MESH
F32 = jnp.float32
BF16 = jnp.bfloat16
I32 = jnp.int32

HD = 128
NEW = 4
HEADS = 3
TOPK = 6
ROOTS = 16
EXPERTS = 32
NY, NZ = 8, 8
NC = NY * NZ
NX = 4
BLOCKS = 16
KEYS = BLOCKS * 128
D = 2560
Q4 = 640
FFP = 384
ROWS = 16
USED = 10
OROWS = 14
QROWS = 12
SLOTS = NC * 2
GRP = Q4 // 128
BIG = 16384.0
UNSEEN = -65536.0
SCALE = 1.0 / math.sqrt(HD)
LOG2E = 1.4426950408889634
SPAN = 512
PACKED = 96
PARTS = ((5, 4, 6, 3), (7, 2, 1, 0))
SRC = 72


def hops(offset):
    return min(offset, 8 - offset)


ORDER = sorted(
    [(dy, dz) for dy in range(NY) for dz in range(NZ) if dy or dz], key=lambda o: -hops(o[0]) - hops(o[1])
)


def iota(shape, dim):
    return lax.broadcasted_iota(I32, shape, dim)


def mm(a, b):
    return jnp.dot(a, b, preferred_element_type=F32)


def mmt(a, b):
    return lax.dot_general(a, b, (((1,), (1,)), ((), ())), preferred_element_type=F32)


def flag(cond):
    return jnp.where(cond, 1.0, 0.0).astype(BF16)


def tile_rows(place, out, lse):
    row, lane = iota((PACKED, 128), 0), iota((PACKED, 128), 1)
    high = lse.astype(BF16).astype(F32)
    mid = (lse - high).astype(BF16).astype(F32)
    own = lane - (row - 12 * ((row * 43) >> 9))
    parts = jnp.where(own == 0, high, jnp.where(own == 16, mid, jnp.where(own == 32, lse - high - mid, 0.0)))
    return mm(place, jnp.concatenate([out.astype(BF16), parts.astype(BF16)], axis=0)).astype(BF16)


def kernel(
    node_hbm, len_hbm, slen_hbm, routes_hbm,
    q_hbm, new_hbm, res_hbm, groot_hbm, rgroup_hbm, gain_hbm,
    suf_hbm, kv_hbm, outw_hbm, router_hbm, wgu_hbm, wd_hbm,
    att_ref, out_ref,
    node_s, len_s, slen_s, routes_s, q_ref, new_ref, res_ref, groot_ref, rgroup_ref, gain_ref,
    qtile, qown, qbuf, kv, feat, nl, freq, scores, rownode, ostage, oland, suf, newkv, atile, outw, router,
    place, gather, lsepick, spreads, pstage, pland, stream, pmat, pback, pick, pack, xland, wgu, wd, gstage, gland, hstage, hland, rstage, rland,
    small_sem, load_sem, core_send, core_recv, q_send, q_recv, o_send, o_recv, p_send, p_recv, x_send, x_recv,
    g_send, g_recv, h_send, h_recv, r_send, r_recv,
):
    x = lax.axis_index("kv")
    blk = lax.axis_index("blk")
    core = lax.rem(blk, 2)
    chip = blk // 2
    y, z = chip // NZ, lax.rem(chip, NZ)
    partner = chip * 2 + (1 - core)

    def plane_peer(c):
        return (x, c * 2 + core)

    rows_y, rows_z = [lax.rem(y + o, NY) * NZ for o in range(NY)], [lax.rem(z + o, NZ) for o in range(NZ)]
    peers = [rows_y[dy] + rows_z[dz] for dy, dz in ORDER]

    smalls = [
        pltpu.make_async_copy(src, dst, small_sem.at[i])
        for i, (src, dst) in enumerate((
            (q_hbm, q_ref), (node_hbm, node_s), (len_hbm, len_s), (groot_hbm, groot_ref), (rgroup_hbm, rgroup_ref),
            (routes_hbm, routes_s), (slen_hbm, slen_s), (new_hbm, new_ref), (res_hbm, res_ref), (gain_hbm, gain_ref),
        ))
    ]
    for copy in smalls:
        copy.start()
    loads = [
        pltpu.make_async_copy(kv_hbm, kv.at[pl.ds(0, KEYS)], load_sem.at[0]),
        pltpu.make_async_copy(suf_hbm, suf, load_sem.at[1]),
        pltpu.make_async_copy(outw_hbm, outw, load_sem.at[2]),
        pltpu.make_async_copy(router_hbm, router, load_sem.at[3]),
        pltpu.make_async_copy(wgu_hbm, wgu.at[0], load_sem.at[4]),
        pltpu.make_async_copy(wd_hbm, wd.at[pl.ds(0, FFP)], load_sem.at[5]),
    ]
    for copy in loads:
        copy.start()

    qbuf[...] = jnp.zeros_like(qbuf)
    oland[...] = jnp.zeros_like(oland)
    xland[...] = jnp.zeros_like(xland)
    rland[...] = jnp.zeros_like(rland)

    barrier = pltpu.get_barrier_semaphore()

    for peer in peers:
        pl.semaphore_signal(barrier, inc=1, device_id=plane_peer(peer), device_id_type=MESH)
    pl.semaphore_signal(barrier, inc=1, device_id=(x, partner), device_id_type=MESH)
    for k in range(1, NX):
        pl.semaphore_signal(barrier, inc=1, device_id=(lax.rem(x + k, NX), blk), device_id_type=MESH)

    for copy in smalls:
        copy.wait()
    qtile[...] = jnp.zeros((ROWS, HD), F32)
    for h in range(HEADS):
        qtile[h * NEW:(h + 1) * NEW, :] = q_ref[:, h * HD:(h + 1) * HD].astype(F32)
    qown[...] = qtile[...].astype(BF16)

    lane8, row8 = iota((8, 128), 1), iota((8, 128), 0)
    table = jnp.where(row8 == 0, -1, 0)
    for b in range(BLOCKS):
        table = jnp.where((lane8 == b) & (row8 == 0), node_s[b], table)
        table = jnp.where((lane8 == b) & (row8 == 1), len_s[b], table)
    nl[0] = table

    pl.semaphore_wait(barrier, NC + NX - 1)

    own_q = pltpu.make_async_copy(qown.at[pl.ds(0, QROWS)], qbuf.at[y, pl.ds(z * ROWS, QROWS)], q_recv.at[y])
    own_q.start()

    for peer in peers:
        pltpu.make_async_remote_copy(
            src_ref=qown.at[pl.ds(0, QROWS)], dst_ref=qbuf.at[y, pl.ds(z * ROWS, QROWS)], send_sem=q_send,
            recv_sem=q_recv.at[y], device_id=plane_peer(peer), device_id_type=MESH,
        ).start()

    def to_partner(src, dst, i):
        return pltpu.make_async_remote_copy(
            src_ref=src, dst_ref=dst, send_sem=core_send.at[i], recv_sem=core_recv.at[i],
            device_id=(x, partner), device_id_type=MESH,
        )

    swaps = [
        to_partner(nl.at[0], nl.at[1], 0),
        to_partner(kv_hbm, kv.at[pl.ds(KEYS, KEYS)], 1),
        to_partner(wgu_hbm, wgu.at[1], 2),
        to_partner(wd_hbm, wd.at[pl.ds(FFP, FFP)], 3),
    ]
    for copy in swaps:
        copy.start()

    sub, lane = iota((128, 128), 0), iota((128, 128), 1)
    groups = groot_ref.shape[1]
    node, group = iota((128, groups), 0), iota((128, groups), 1)
    group_node = jnp.where((node == groot_ref[...]) | (node == group + ROOTS), BIG, 0.0).astype(BF16)
    in_group = flag(iota((groups, 128), 0) == rgroup_ref[...])
    freq[...] = mm(group_node, in_group).astype(BF16)

    esub, elane = iota((EXPERTS, 128), 0), iota((EXPERTS, 128), 1)
    seen = jnp.zeros((EXPERTS, 128), I32)
    places = [jnp.zeros((EXPERTS, 128), F32), jnp.zeros((EXPERTS, 128), F32)]
    trow, tlane = iota((8, EXPERTS), 0), iota((8, EXPERTS), 1)
    named = jnp.zeros((8, EXPERTS), I32)
    ranked = jnp.zeros((8, EXPERTS), I32)
    for t in range(NEW):
        hit = esub == routes_s[t, 0]
        row_hit = tlane == routes_s[t, 0]
        for k in range(1, TOPK):
            hit = hit | (esub == routes_s[t, k])
            row_hit = row_hit | (tlane == routes_s[t, k])
        for c in range(2):
            places[c] = jnp.where(hit & (seen == c) & ((elane & 7) == t) & (elane < 8 * GRP), 1.0, places[c])
        seen = seen + jnp.where(hit, 1, 0)
        named = named + jnp.where(row_hit & (trow == t), 1, 0)
        ranked = ranked + jnp.where(row_hit & (trow > t), 1, 0)
    prow, plane = iota((EXPERTS * ROWS, 128), 0), iota((EXPERTS * ROWS, 128), 1)
    spread = flag(iota((EXPERTS * ROWS, EXPERTS), 0) >> 4 == iota((EXPERTS * ROWS, EXPERTS), 1))
    same = (prow & 15) >> 1 == plane >> 3
    choose = jnp.where(same & ((prow & 1) == 0), mm(spread, places[0].astype(BF16)), 0.0)
    choose = jnp.where(same & ((prow & 1) == 1), mm(spread, places[1].astype(BF16)), choose)
    pick[...] = choose.astype(BF16)

    s, c = iota((GRP * 32, 256), 0), iota((GRP * 32, 256), 1)
    pmat[...] = flag(c == ((s & 31) >> 1) * ROWS + (s >> 5) * 2 + (s & 1))
    c, s = iota((256, GRP * 32), 0), iota((256, GRP * 32), 1)
    pback[...] = flag(c == ((s & 31) >> 1) * ROWS + (s >> 5) * 2 + (s & 1))

    p, r = iota((PACKED, 128), 0), iota((PACKED, 128), 1)
    gather[...] = flag(((r & 15) < 12) & (p == (r >> 4) * 12 + (r & 15)))
    r, p = iota((128, PACKED), 0), iota((128, PACKED), 1)
    tile = (p * 43) >> 9
    place[...] = jnp.concatenate([flag(r == tile * 4 + p)] + [flag(r == tile * 16 + 12)], axis=1)
    for o in range(NY):
        request = (lax.rem(y + o, NY) * NZ + ((iota((PACKED, 128), 0) * 43) >> 9)) * 2 + core
        rownode[o] = mmt(flag(request == iota((PACKED, 128), 1)), freq[...]).astype(BF16)
    msrc, mcol = iota((SRC, SRC * ROWS), 0), iota((SRC, SRC * ROWS), 1)
    lsepick[...] = flag((mcol >> 4 == msrc) & ((mcol & 15) == 12))
    spreads[...] = flag(iota((128, SRC * ROWS), 1) >> 4 == iota((128, SRC * ROWS), 0))

    loads[1].wait()
    newkv[...] = jnp.zeros((128, 2 * HD), F32)
    newkv[0:NEW, :] = new_ref[...].astype(F32)
    fresh = newkv[...].astype(BF16)
    q16 = qown[...]
    srow, slane = iota((ROWS, 128), 0), iota((ROWS, 128), 1)
    s_suffix = jnp.where(slane < slen_s[0], mmt(q16, suf[:, :HD]) * SCALE, UNSEEN)
    s_fresh = jnp.where(slane <= (srow & 3), mmt(q16, fresh[:, :HD]) * SCALE, UNSEEN)
    s_top = jnp.maximum(jnp.max(s_suffix, axis=1, keepdims=True), jnp.max(s_fresh, axis=1, keepdims=True))
    w_suffix = jnp.exp(s_suffix - s_top).astype(BF16)
    w_fresh = jnp.exp(s_fresh - s_top).astype(BF16)
    s_sum = jnp.sum(w_suffix.astype(F32), axis=1, keepdims=True) + jnp.sum(w_fresh.astype(F32), axis=1, keepdims=True)
    s_out = (mm(w_suffix, suf[:, HD:]) + mm(w_fresh, fresh[:, HD:])) / s_sum
    s_lse = jnp.broadcast_to(s_top + jnp.log(s_sum), (ROWS, HD))
    pad = jnp.zeros((PACKED - ROWS, HD), F32)
    s_out, s_lse = jnp.where(srow < 12, s_out, 0.0), jnp.where(srow < 12, s_lse, 0.0)
    own_tiles = tile_rows(
        place[...], jnp.concatenate([s_out, pad], axis=0), jnp.concatenate([s_lse, pad], axis=0)
    )

    def features(part):
        node_hot = flag(sub == nl[part, 0:1, :])
        lengths = jnp.broadcast_to(nl[part, 1:2, :], (128, 128)).astype(F32).astype(BF16)
        for i in range(KEYS // SPAN):
            key, block = iota((SPAN, 128), 0) + i * SPAN, iota((SPAN, 128), 1)
            member = flag(key >> 7 == block)
            used = (key & 127).astype(F32) < mmt(member, lengths)
            feat[part * KEYS + i * SPAN:part * KEYS + (i + 1) * SPAN, :] = jnp.where(
                used, mmt(member, node_hot), 0.0
            ).astype(BF16)

    features(0)
    swaps[0].wait()
    features(1)
    loads[0].wait()
    swaps[1].wait()

    spans = [slice(i * SPAN, (i + 1) * SPAN) for i in range(2 * KEYS // SPAN)]
    part_rows = len(PARTS[0]) * PACKED

    def part_query(offsets):
        rows = []
        for o in offsets:
            yy = lax.rem(y + o, NY)
            row = qbuf.at[yy, pl.ds(0, NZ * QROWS)]
            pltpu.make_async_copy(row, row, q_recv.at[yy]).wait()
            rows.append(jnp.concatenate([mm(gather[...], qbuf[yy]).astype(BF16), rownode[o]], axis=1))
        return jnp.concatenate(rows, axis=0)

    def send_part(offsets, best, total):
        norm = total[:, HD:]
        result = total[:, :HD] / norm
        lse = jnp.where(best > 0.5 * BIG, (best - BIG) * SCALE + jnp.log(norm), UNSEEN)
        for i, o in enumerate(offsets):
            rows = slice(i * PACKED, (i + 1) * PACKED)
            ostage[lax.rem(y + o, NY)] = tile_rows(place[...], result[rows], lse[rows])
        for dy, dz in ORDER:
            if dy in offsets:
                pltpu.make_async_remote_copy(
                    src_ref=ostage.at[lax.rem(y + dy, NY), pl.ds(lax.rem(z + dz, NZ) * ROWS, OROWS)],
                    dst_ref=oland.at[pl.ds(chip * ROWS, OROWS)], send_sem=o_send, recv_sem=o_recv,
                    device_id=plane_peer(rows_y[dy] + rows_z[dz]), device_id_type=MESH,
                ).start()
        if 0 in offsets:
            pltpu.make_async_copy(
                ostage.at[y, pl.ds(z * ROWS, OROWS)], oland.at[pl.ds(chip * ROWS, OROWS)], o_recv
            ).start()

    ones = jnp.ones((SPAN, HD), BF16)
    before = None
    for step in range(len(PARTS) + 1):
        now = step < len(PARTS)
        if now:
            query = part_query(PARTS[step])
            top = jnp.full((part_rows, 128), -3e38, F32)
        if before is not None:
            halves = [slice(0, part_rows // 2), slice(part_rows // 2, part_rows)]
            totals = [jnp.zeros((part_rows // 2, 2 * HD), F32)] * 2
        for span in spans:
            if now:
                s = mmt(query, jnp.concatenate([kv[span, :HD], feat[span, :]], axis=1))
                scores[step, :, span] = s
                for j in range(SPAN // 128):
                    top = jnp.maximum(top, s[:, j * 128:(j + 1) * 128])
            if before is not None:
                value = jnp.concatenate([kv[span, HD:], ones], axis=1)
                for i, half in enumerate(halves):
                    weight = jnp.exp2((scores[step - 1, half, span] - before[half]) * (SCALE * LOG2E)).astype(BF16)
                    totals[i] = totals[i] + mm(weight, value)
        if before is not None:
            send_part(PARTS[step - 1], before, jnp.concatenate(totals, axis=0))
        before = jnp.max(top, axis=1, keepdims=True) if now else None

    arrived = oland.at[pl.ds(0, NC * OROWS)]
    pltpu.make_async_copy(arrived, arrived, o_recv).wait()
    tiles = jnp.concatenate([oland[...], own_tiles], axis=0)
    lses = mm(lsepick[...], tiles)
    lses = lses + pltpu.roll(lses, 112, 1) + pltpu.roll(lses, 96, 1)
    lses = jnp.where(iota((SRC, 128), 0) < NC + 1, lses, UNSEEN)
    share = jnp.exp(lses - jnp.max(lses, axis=0, keepdims=True))
    share = share / jnp.sum(share, axis=0, keepdims=True)
    share = jnp.transpose(jnp.concatenate([share, jnp.zeros((128 - SRC, 128), F32)], axis=0))[0:ROWS]
    share_high = share.astype(BF16)
    share_low = (share - share_high.astype(F32)).astype(BF16)
    shares = jnp.concatenate([share_high, share_low], axis=0)
    wide = mm(shares, spreads[...])
    mixed = jnp.where(
        (iota((2 * ROWS, SRC * ROWS), 1) & 15) == (iota((2 * ROWS, SRC * ROWS), 0) & 15), wide, 0.0
    ).astype(BF16)
    merged = mm(mixed, tiles)
    atile[...] = merged[0:ROWS] + merged[ROWS:]
    for h in range(HEADS):
        att_ref[:, h * HD:(h + 1) * HD] = atile[h * NEW:(h + 1) * NEW, :].astype(BF16)

    loads[2].wait()
    pstage[...] = mm(att_ref[...], outw[...]).astype(BF16)
    own_p = pltpu.make_async_copy(pstage, pland.at[x], p_recv)
    own_p.start()
    for k in (2, 1, 3):
        pltpu.make_async_remote_copy(
            src_ref=pstage, dst_ref=pland.at[x], send_sem=p_send, recv_sem=p_recv,
            device_id=(lax.rem(x + k, NX), blk), device_id_type=MESH,
        ).start()
    stream[...] = jnp.zeros((8, D), F32)
    loads[3].wait()
    pltpu.make_async_copy(pland, pland, p_recv).wait()
    summed = pland[0].astype(F32) + pland[1].astype(F32) + pland[2].astype(F32) + pland[3].astype(F32)
    stream[0:NEW, :] = res_ref[...].astype(F32) + summed
    full = stream[...]
    inverse = lax.rsqrt(jnp.mean(full * full, axis=1, keepdims=True) + 1e-6)
    normed = full * inverse * gain_ref[...].reshape(1, D)
    quarter = pl.ds(pl.multiple_of(x * Q4, 128), Q4)
    own_stream = stream[:, quarter]
    own_normed = own_stream * inverse * gain_ref[quarter].reshape(1, Q4)

    groups = [own_normed[:, g * 128:(g + 1) * 128] for g in range(GRP)]
    packed = jnp.concatenate(groups + [jnp.zeros((128 - 8 * GRP, 128), F32)], axis=0).astype(BF16)
    pack[...] = mm(pick[...], packed).astype(BF16)
    land = pl.ds(chip * ROWS, USED)
    pltpu.make_async_copy(pack.at[pl.ds((chip // 2) * ROWS, USED)], xland.at[land], x_recv).start()

    for peer in peers:
        pltpu.make_async_remote_copy(
            src_ref=pack.at[pl.ds((peer // 2) * ROWS, USED)], dst_ref=xland.at[land], send_sem=x_send,
            recv_sem=x_recv, device_id=plane_peer(peer), device_id_type=MESH,
        ).start()

    logits = mmt(normed.astype(BF16), router[...])
    gate = jnp.where(named > 0, 1.0 / (1.0 + jnp.exp(-logits)), 0.0)
    gate = gate / jnp.where(trow[:, 0:1] < NEW, jnp.sum(gate, axis=1, keepdims=True), 1.0)
    owner = flag(iota((EXPERTS, NC * ROWS), 1) >> 5 == iota((EXPERTS, NC * ROWS), 0))
    acol, arow = iota((GRP * ROWS, NC * ROWS), 1), iota((GRP * ROWS, NC * ROWS), 0)
    mixer = jnp.zeros((GRP * ROWS, NC * ROWS), F32)
    for c in range(2):
        slot_gate = jnp.where(ranked == c, gate, 0.0)
        high = slot_gate.astype(BF16).astype(F32)
        both = jnp.concatenate([high, slot_gate - high], axis=0).astype(BF16)
        spreaded = mm(jnp.concatenate([both] * GRP, axis=0), owner)
        mixer = jnp.where((acol & 15) == (arow >> 4) * 2 + c, spreaded, mixer)
    mixer = mixer.astype(BF16)

    loads[4].wait()
    swaps[2].wait()
    got = pl.ds(0, NC * USED)
    pltpu.make_async_copy(xland.at[got], xland.at[got], x_recv).wait()
    blocks = []
    for b in range(4):
        slots = mm(pmat[...], xland[b * 256:(b + 1) * 256, :]).astype(BF16)
        blocks.append(jnp.concatenate([slots[g * 32:(g + 1) * 32] for g in range(GRP)], axis=1))
    tokens = jnp.concatenate(blocks, axis=0)
    part = SLOTS // NX
    mine = pl.ds(x * part, part)
    for p in range(2):
        gstage[p] = mm(tokens, wgu[p]).astype(BF16)
        pltpu.make_async_copy(gstage.at[p, mine], gland.at[p, x], g_recv.at[p]).start()
        for k in (2, 1, 3):
            peer = lax.rem(x + k, NX)
            pltpu.make_async_remote_copy(
                src_ref=gstage.at[p, pl.ds(peer * part, part)], dst_ref=gland.at[p, x], send_sem=g_send.at[p],
                recv_sem=g_recv.at[p], device_id=(peer, blk), device_id_type=MESH,
            ).start()
    for p in range(2):
        pltpu.make_async_copy(gland.at[p], gland.at[p], g_recv.at[p]).wait()
        gate_up = gland[p, 0].astype(F32) + gland[p, 1].astype(F32) + gland[p, 2].astype(F32) + gland[p, 3].astype(F32)
        gates, ups = gate_up[:, :FFP], gate_up[:, FFP:]
        hstage[p] = (gates / (1.0 + jnp.exp(-gates)) * ups).astype(BF16)
        pltpu.make_async_copy(hstage.at[p], hland.at[p, mine], h_recv.at[p]).start()
        for k in (2, 1, 3):
            pltpu.make_async_remote_copy(
                src_ref=hstage.at[p], dst_ref=hland.at[p, mine], send_sem=h_send.at[p], recv_sem=h_recv.at[p],
                device_id=(lax.rem(x + k, NX), blk), device_id_type=MESH,
            ).start()
    loads[5].wait()
    swaps[3].wait()
    down = jnp.zeros((SLOTS, Q4), F32)
    for p in range(2):
        pltpu.make_async_copy(hland.at[p], hland.at[p], h_recv.at[p]).wait()
        down = down + mm(hland[p], wd[p * FFP:(p + 1) * FFP, :])
    down = down.astype(BF16)
    for b in range(4):
        rows = [down[b * 32:(b + 1) * 32, g * 128:(g + 1) * 128] for g in range(GRP)]
        rstage[b * 256:(b + 1) * 256, :] = mm(pback[...], jnp.concatenate(rows, axis=0)).astype(BF16)
    pltpu.make_async_copy(rstage.at[land], rland.at[land], r_recv).start()

    for peer in peers:
        pltpu.make_async_remote_copy(
            src_ref=rstage.at[pl.ds(peer * ROWS, USED)], dst_ref=rland.at[land], send_sem=r_send,
            recv_sem=r_recv, device_id=plane_peer(peer), device_id_type=MESH,
        ).start()
    pltpu.make_async_copy(rland.at[got], rland.at[got], r_recv).wait()
    experts = mm(mixer, rland[...])
    for g in range(GRP):
        both = experts[g * ROWS:g * ROWS + 8] + experts[g * ROWS + 8:(g + 1) * ROWS]
        out_ref[:, g * 128:(g + 1) * 128] = (own_stream[:, g * 128:(g + 1) * 128] + both)[0:NEW].astype(BF16)

    def sent(ref, sem):
        pltpu.make_async_copy(ref, ref, sem).wait()

    sent(oland.at[pl.ds(0, (NC - 1) * QROWS)], q_send)
    sent(oland.at[pl.ds(0, (NC - 1) * OROWS)], o_send)
    few = pl.ds(0, (NC - 1) * USED)
    sent(oland.at[few], x_send)
    sent(oland.at[few], r_send)
    sent(pland.at[pl.ds(0, NX - 1)], p_send)
    for p in range(2):
        sent(gland.at[p, pl.ds(0, NX - 1)], g_send.at[p])
        sent(hland.at[p, pl.ds(0, (NX - 1) * part)], h_send.at[p])


def hand_on(att_ref, out_ref, att_out, layer_out):
    att_out[...] = att_ref[...]
    layer_out[...] = out_ref[...]


def local(
    residual, queries, new_kv, suffix_kv, suffix_len, shared_kv, block_node, block_len, group_root, request_group,
    out_weight, norm_gain, router, routes, expert_gate_up, expert_down,
):
    vmem = pl.BlockSpec(memory_space=pltpu.VMEM)
    hbm = pl.BlockSpec(memory_space=pl.ANY)
    dma = pltpu.SemaphoreType.DMA
    results = pl.pallas_call(
        kernel,
        out_shape=(jax.ShapeDtypeStruct((NEW, HEADS * HD), BF16), jax.ShapeDtypeStruct((NEW, Q4), BF16)),
        in_specs=[hbm] * 16,
        out_specs=(vmem, vmem),
        scratch_shapes=[
            pltpu.SMEM(block_node.shape, I32),
            pltpu.SMEM(block_len.shape, I32),
            pltpu.SMEM(suffix_len.shape, I32),
            pltpu.SMEM(routes.shape, I32),
            pltpu.VMEM(queries.shape, BF16),
            pltpu.VMEM(new_kv.shape, BF16),
            pltpu.VMEM(residual.shape, BF16),
            pltpu.VMEM((1, group_root.shape[0]), I32),
            pltpu.VMEM((1, 128), I32),
            pltpu.VMEM((D,), F32),
            pltpu.VMEM((ROWS, HD), F32),
            pltpu.VMEM((ROWS, HD), BF16),
            pltpu.VMEM((NY, NZ * ROWS, HD), BF16),
            pltpu.VMEM((2 * KEYS, 2 * HD), BF16),
            pltpu.VMEM((2 * KEYS, 128), BF16),
            pltpu.VMEM((2, 8, 128), I32),
            pltpu.VMEM((128, 128), BF16),
            pltpu.VMEM((len(PARTS), len(PARTS[0]) * PACKED, 2 * KEYS), F32),
            pltpu.VMEM((NY, PACKED, 128), BF16),
            pltpu.VMEM((NY, NZ * ROWS, HD), BF16),
            pltpu.VMEM((NC * ROWS, HD), BF16),
            pltpu.VMEM((128, 2 * HD), BF16),
            pltpu.VMEM((128, 2 * HD), F32),
            pltpu.VMEM((ROWS, HD), F32),
            pltpu.VMEM((HEADS * HD, D), BF16),
            pltpu.VMEM((EXPERTS, D), BF16),
            pltpu.VMEM((128, 2 * PACKED), BF16),
            pltpu.VMEM((PACKED, 128), BF16),
            pltpu.VMEM((SRC, SRC * ROWS), BF16),
            pltpu.VMEM((128, SRC * ROWS), BF16),
            pltpu.VMEM((NEW, D), BF16),
            pltpu.VMEM((NX, NEW, D), BF16),
            pltpu.VMEM((8, D), F32),
            pltpu.VMEM((GRP * 32, 256), BF16),
            pltpu.VMEM((256, GRP * 32), BF16),
            pltpu.VMEM((EXPERTS * ROWS, 128), BF16),
            pltpu.VMEM((EXPERTS * ROWS, 128), BF16),
            pltpu.VMEM((NC * ROWS, 128), BF16),
            pltpu.VMEM((2, Q4, 2 * FFP), BF16),
            pltpu.VMEM((2 * FFP, Q4), BF16),
            pltpu.VMEM((2, SLOTS, 2 * FFP), BF16),
            pltpu.VMEM((2, NX, SLOTS // NX, 2 * FFP), BF16),
            pltpu.VMEM((2, SLOTS // NX, FFP), BF16),
            pltpu.VMEM((2, SLOTS, FFP), BF16),
            pltpu.VMEM((NC * ROWS, 128), BF16),
            pltpu.VMEM((NC * ROWS, 128), BF16),
            dma((10,)), dma((6,)), dma((4,)), dma((4,)), dma, dma((NY,)), dma, dma, dma, dma, dma, dma,
            dma((2,)), dma((2,)), dma((2,)), dma((2,)), dma, dma,
        ],
        compiler_params=pltpu.CompilerParams(collective_id=0, has_side_effects=True, vmem_limit_bytes=60 * 1024 * 1024),
        name="decode_step",
    )(
        block_node, block_len, suffix_len, routes,
        queries, new_kv, residual, group_root.reshape(1, -1), request_group.reshape(1, -1), norm_gain,
        suffix_kv.reshape(128, 2 * HD), shared_kv.reshape(KEYS, 2 * HD), out_weight, router.T,
        expert_gate_up.reshape(Q4, 2 * FFP), expert_down.reshape(FFP, Q4),
    )
    return pl.pallas_call(
        hand_on,
        out_shape=(jax.ShapeDtypeStruct((NEW, HEADS * HD), BF16), jax.ShapeDtypeStruct((NEW, Q4), BF16)),
        in_specs=[vmem] * 2,
        out_specs=(vmem, vmem),
        name="hand_on",
    )(*results)


def solution(mesh):
    in_specs = (
        P("blk", None),
        P("blk", "kv"),
        P("blk", "kv"),
        P("blk", "kv", None, None),
        P("blk"),
        P("blk", "kv", None, None),
        P("blk"),
        P("blk"),
        P(),
        P(),
        P("kv", None),
        P(),
        P(),
        P("blk", None),
        P("blk", "kv", None),
        P("blk", None, "kv"),
    )
    out_specs = (P("blk", "kv"), P("blk", "kv"))
    return jax.shard_map(local, mesh=mesh, in_specs=in_specs, out_specs=out_specs, check_vma=False)
```
